32 devices in a mesh: space: 4 (over y, core), energy: 8 (over z, x).
Axes of the slice: x: 2, y: 2, z: 4, core: 2. Of those that a mesh axis runs over, the one named last changes fastest.
Arguments:
- onsite: float32 [2, 8, 64, 64], P(None, 'space'), as said below
- hopping: float32 [2, 8, 64, 64], P(None, 'space'), may hold values from -0.375 to 0.375
- sigma_prior: float32 [2, 8, 8, 64, 64], P(None, 'energy', 'space'), as said below
- screened: float32 [2, 15, 32768], P(None, None, ('space', 'energy')), may hold values from -6 to 6
Outputs:
- sigma_next: float32 [2, 8, 32768], P(None, None, ('space', 'energy'))
The draws below stay inside these ranges and needn't reach their ends.
Inputs may be any that keep to these rules, and one draw needn't show every extreme that they name: `onsite`: every block is Hermitian: real part symmetric, imaginary part antisymmetric. `sigma_prior`: every block is Hermitian: real part symmetric, imaginary part antisymmetric.
All inputs are finite; a program needn't handle non-finite values.
Results may differ from the reference program's by a relative error of at most 0.0003.
Values sent between devices are 32-bit elements; how exact they have to be, the bound alone decides.
No kernel may reach another device: no remote copies, remote signals or barrier semaphores. Data moves between devices by JAX's collectives and lax.ppermute only.
A program may use at most 128 MiB of HBM per device.

```python
import jax
import jax.numpy as jnp
from jax import lax

B = 64
NB = 8
NE = 8
LAGS = 15


def hermitian_blocks(key, dimensions, spread):
    key_real, key_imag = jax.random.split(key)
    real_draw = jax.random.normal(key_real, dimensions, jnp.float32)
    imag_draw = jax.random.normal(key_imag, dimensions, jnp.float32)
    factor = spread / B ** 0.5
    real_part = 0.5 * factor * (real_draw + jnp.swapaxes(real_draw, -1, -2))
    imag_part = 0.5 * factor * (imag_draw - jnp.swapaxes(imag_draw, -1, -2))
    return jnp.stack([real_part, imag_part])


def draw_onsite(key, part):
    return hermitian_blocks(jax.random.fold_in(key, 11), (NB, B, B), 1.0)


def draw_sigma_prior(key, part):
    return hermitian_blocks(jax.random.fold_in(key, 23), (NE, NB, B, B), 0.5)


def shard_levels(own_key, dims, cuts, least, largest):
    factor_of, own = 1.0, jax.random.fold_in(own_key, 6)
    for position, parts in cuts:
        heights = jnp.exp(jax.random.uniform(jax.random.fold_in(own, position), (parts,), jnp.float32, least / len(cuts), largest / len(cuts)))
        factor_of = factor_of * jnp.repeat(heights, dims[position] // parts).reshape([-1 if axis == position else 1 for axis in range(len(dims))])
    return factor_of


def normal_values(key, extent, scale, reach, shards=(), kind=jnp.bfloat16):
    level = shard_levels(key, extent, shards, -0.22, 0.18) if shards else 1.0
    drawn = jax.random.normal(key, extent, jnp.float32) * scale * level
    return jnp.minimum(jnp.maximum(drawn, -reach), reach).astype(kind)


def setup_inputs(seed: int = 0) -> dict:
    splits = jax.random.split(jax.random.key(seed), 5)
    onsite = draw_onsite(jax.random.fold_in(splits[4], 71), 0)
    hopping = normal_values(splits[1], (2, NB, B, B), (4 * B) ** -0.5, 0.375, ((1, 4),), jnp.float32)
    sigma_prior = draw_sigma_prior(jax.random.fold_in(splits[4], 71), 0)
    screened = normal_values(splits[3], (2, LAGS, NB * B * B), 1.0, 6.0, ((2, 32),), jnp.float32)
    return dict(onsite=onsite, hopping=hopping, sigma_prior=sigma_prior, screened=screened)


broadening = 0.25
energy_low = -3.0
energy_high = 3.0

def complex_product(left_factor, right_factor):
    real_part = jnp.matmul(left_factor[0], right_factor[0], precision=lax.Precision.HIGHEST) - jnp.matmul(left_factor[1], right_factor[1], precision=lax.Precision.HIGHEST)
    imag_part = jnp.matmul(left_factor[0], right_factor[1], precision=lax.Precision.HIGHEST) + jnp.matmul(left_factor[1], right_factor[0], precision=lax.Precision.HIGHEST)
    return jnp.stack([real_part, imag_part])

def adjoint(matrix):
    return jnp.stack([jnp.swapaxes(matrix[0], -1, -2), -jnp.swapaxes(matrix[1], -1, -2)])

def invert(matrix):
    orbitals = matrix.shape[-1]
    upper_half = jnp.concatenate([matrix[0], -matrix[1]], axis=1)
    lower_half = jnp.concatenate([matrix[1], matrix[0]], axis=1)
    inverse = jnp.linalg.inv(jnp.concatenate([upper_half, lower_half], axis=0))
    return jnp.stack([inverse[:orbitals, :orbitals], inverse[orbitals:, :orbitals]])

def chain_green(onsite, coupling, sigma_slice, energy):
    identity = jnp.eye(B, dtype=jnp.float32)
    system = jnp.stack([energy * identity - onsite[0] - sigma_slice[0], broadening * identity - onsite[1] - sigma_slice[1]])
    system_seq = jnp.moveaxis(system, 1, 0)
    coupling_seq = jnp.moveaxis(coupling, 1, 0)
    previous_seq = jnp.concatenate([jnp.zeros_like(coupling_seq[:1]), coupling_seq[:-1]], axis=0)
    nothing = jnp.zeros((2, B, B), jnp.float32)

    def left_step(carried, pieces):
        system_here, coupling_here = pieces
        inverse = invert(system_here - carried)
        return (complex_product(complex_product(adjoint(coupling_here), inverse), coupling_here), carried)
    unused_left, left_seq = lax.scan(left_step, nothing, (system_seq, coupling_seq))

    def right_step(carried, pieces):
        system_here, previous_here = pieces
        inverse = invert(system_here - carried)
        return (complex_product(complex_product(previous_here, inverse), adjoint(previous_here)), carried)
    unused_right, right_seq = lax.scan(right_step, nothing, (system_seq, previous_seq), reverse=True)
    return jax.vmap(invert)(system_seq - left_seq - right_seq)

def reference(onsite, hopping, sigma_prior, screened):
    active = (jnp.arange(NB) < NB - 1).astype(jnp.float32)
    coupling = hopping * active[None, :, None, None]
    energies = energy_low + (energy_high - energy_low) * (jnp.arange(NE).astype(jnp.float32) + 0.5) / NE
    sigma_seq = jnp.moveaxis(sigma_prior, 1, 0)

    def one_energy(pieces):
        sigma_slice, energy = pieces
        return chain_green(onsite, coupling, sigma_slice, energy)
    green_all = lax.map(one_energy, (sigma_seq, energies))
    green_flat = green_all.reshape(NE, NB, 2, B * B)
    green_blocks = jnp.transpose(green_flat, (1, 2, 0, 3))
    screen_blocks = jnp.transpose(screened.reshape(2, LAGS, NB, B * B), (2, 0, 1, 3))

    def convolve(pieces):
        green_here, screen_here = pieces
        green_complex = green_here[0] + 1j * green_here[1]
        screen_complex = screen_here[0] + 1j * screen_here[1]
        spectrum = jnp.fft.fft(green_complex, n=LAGS, axis=0) * jnp.fft.fft(screen_complex, axis=0)
        values = jnp.fft.ifft(spectrum, axis=0)[:NE]
        return jnp.stack([jnp.real(values), jnp.imag(values)])
    result = lax.map(convolve, (green_blocks, screen_blocks))
    ordered = jnp.transpose(result, (1, 2, 0, 3)).astype(jnp.float32)
    return ordered.reshape(2, NE, NB * B * B)
```

```python
import functools

import jax
import jax.numpy as jnp
from jax import lax
from jax.experimental import pallas as pl
from jax.experimental.pallas import tpu as pltpu
from jax.sharding import PartitionSpec as P

broadening = 0.25
energy_low = -3.0
energy_high = 3.0

PANEL = 8
SMALL = 2.0**-64
LARGE = 2.0**120


def iota(shape, dim):
    return lax.broadcasted_iota(jnp.int32, shape, dim)


def swap_halves(x):
    return pltpu.roll(x, x.shape[1] // 2, 1)


def low_half(x):
    return iota(x.shape, 1) < x.shape[1] // 2


def lane_broadcast(x, column):
    half = x.shape[1] // 2
    index = (iota(x.shape, 1) & half) + column
    return jnp.take_along_axis(x, index, axis=1, mode="promise_in_bounds")


def sublane_broadcast(x, row):
    return jnp.broadcast_to(x[row : row + 1, :], x.shape)


def complex_reciprocal(real, imag):
    square = real * real + imag * imag
    factor = 1.0 / square
    real_small, imag_small = real * SMALL, imag * SMALL
    factor_small = SMALL / (real_small * real_small + imag_small * imag_small)
    plain = square < LARGE
    return (
        jnp.where(plain, real * factor, real_small * factor_small),
        -jnp.where(plain, imag * factor, imag_small * factor_small),
    )


def invert_block(real, imag):
    real, imag = list(real), list(imag)
    sub = iota(real[0].shape, 0)
    for step in range(PANEL):
        here = sub == step
        pivot_real = sublane_broadcast(real[step], step)
        pivot_imag = sublane_broadcast(imag[step], step)
        recip_real, recip_imag = complex_reciprocal(pivot_real, pivot_imag)
        mult_real = real[step] * recip_real - imag[step] * recip_imag
        mult_imag = real[step] * recip_imag + imag[step] * recip_real
        mult_real = jnp.where(here, -recip_real, mult_real)
        mult_imag = jnp.where(here, -recip_imag, mult_imag)
        for other in range(PANEL):
            if other == step:
                continue
            row_real = sublane_broadcast(real[other], step)
            row_imag = sublane_broadcast(imag[other], step)
            rest_real = jnp.where(here, 0.0, real[other])
            rest_imag = jnp.where(here, 0.0, imag[other])
            real[other] = rest_real - mult_real * row_real + mult_imag * row_imag
            imag[other] = rest_imag - mult_real * row_imag - mult_imag * row_real
        real[step], imag[step] = -mult_real, -mult_imag
    return real, imag


def eliminate_panel(real, imag, panel):
    half = real[0].shape[1] // 2
    lane = iota(real[0].shape, 1) & (half - 1)
    inside = (lane // PANEL) == panel
    unit = jnp.where((lane & (PANEL - 1)) == iota(real[0].shape, 0), 1.0, 0.0)

    def columns(group):
        return (
            [lane_broadcast(real[group], panel * PANEL + c) for c in range(PANEL)],
            [lane_broadcast(imag[group], panel * PANEL + c) for c in range(PANEL)],
        )

    inverse_real, inverse_imag = invert_block(*columns(panel))
    top_real = jnp.where(inside, unit, real[panel])
    top_imag = jnp.where(inside, 0.0, imag[panel])
    row_real = row_imag = None
    for c in range(PANEL):
        a, b = sublane_broadcast(top_real, c), sublane_broadcast(top_imag, c)
        term_real = inverse_real[c] * a - inverse_imag[c] * b
        term_imag = inverse_real[c] * b + inverse_imag[c] * a
        row_real = term_real if row_real is None else row_real + term_real
        row_imag = term_imag if row_imag is None else row_imag + term_imag
    spread_real = [sublane_broadcast(row_real, c) for c in range(PANEL)]
    spread_imag = [sublane_broadcast(row_imag, c) for c in range(PANEL)]
    new_real, new_imag = list(real), list(imag)
    for ahead in range(1, len(real)):
        group = (panel + ahead) % len(real)
        column_real, column_imag = columns(group)
        a = jnp.where(inside, 0.0, real[group])
        b = jnp.where(inside, 0.0, imag[group])
        for c in range(PANEL):
            a = a - column_real[c] * spread_real[c] + column_imag[c] * spread_imag[c]
            b = b - column_real[c] * spread_imag[c] - column_imag[c] * spread_real[c]
        new_real[group], new_imag[group] = a, b
    new_real[panel], new_imag[panel] = row_real, row_imag
    return new_real, new_imag


def invert_pair(first, second):
    low = low_half(first)
    real = jnp.where(low, first, swap_halves(second))
    imag = jnp.where(low, swap_halves(first), second)
    groups = first.shape[0] // PANEL
    real = [real[PANEL * g : PANEL * (g + 1)] for g in range(groups)]
    imag = [imag[PANEL * g : PANEL * (g + 1)] for g in range(groups)]
    for panel in range(groups):
        real, imag = eliminate_panel(real, imag, panel)
    return jnp.concatenate(real, 0), jnp.concatenate(imag, 0)


def side_of_pair(real, imag):
    low = low_half(real)
    return jnp.where(low, real, swap_halves(imag)), jnp.where(low, swap_halves(real), imag)


def times_i(x):
    turned = swap_halves(x)
    return jnp.where(low_half(x), -turned, turned)


def matmul(a, b):
    a_high, b_high = a.astype(jnp.bfloat16), b.astype(jnp.bfloat16)
    a_low = (a - a_high.astype(jnp.float32)).astype(jnp.bfloat16)
    b_low = (b - b_high.astype(jnp.float32)).astype(jnp.bfloat16)
    return jnp.dot(
        jnp.concatenate([a_high, a_high, a_low], 1),
        jnp.concatenate([b_high, b_low, b_high], 0),
        preferred_element_type=jnp.float32,
    )


def pair_solve(real, imag, right_first, right_second):
    low = low_half(real)
    left = jnp.concatenate(
        [
            jnp.concatenate([jnp.where(low, real, 0.0), jnp.where(low, imag, 0.0)], 1),
            jnp.concatenate([jnp.where(low, 0.0, real), jnp.where(low, 0.0, imag)], 1),
        ],
        0,
    )
    rows = real.shape[0]
    firsts, seconds = [], []
    for a, b in zip(right_first, right_second):
        stacked = jnp.concatenate([a, b], 0)
        turned = times_i(stacked)
        right = jnp.concatenate(
            [
                jnp.concatenate([stacked, turned], 1),
                jnp.concatenate([turned, -stacked], 1),
            ],
            0,
        )
        product = matmul(left, right)
        width = stacked.shape[1]
        firsts.append(jnp.concatenate([product[:rows, :width], product[:rows, width:]], 0))
        seconds.append(jnp.concatenate([product[rows:, :width], product[rows:, width:]], 0))
    return jnp.concatenate(firsts, 1), jnp.concatenate(seconds, 1)


def eliminate(block_first, block_second, sides_first, sides_second):
    real, imag = invert_pair(block_first, block_second)
    right_first, right_second = pair_solve(
        real,
        imag,
        [sides_first[1], sides_first[2]],
        [sides_second[1], sides_second[2]],
    )
    results = []
    for sides, right in ((sides_first, right_first), (sides_second, right_second)):
        rows, width = sides[0].shape
        out = matmul(jnp.concatenate([sides[0], sides[3]], 0), right)
        results.append(
            (out[:rows, :width], out[:rows, width:], out[rows:, :width], out[rows:, width:])
        )
    return results


def adjoint(x):
    half = x.shape[1] // 2
    turned = x.T
    return jnp.concatenate([turned[:half], -turned[half:]], 1)


def reduce_kernel(
    energy_ref, onsite_ref, hopping_ref, sigma_ref, own_ref, reduced_ref
):
    orbitals = onsite_ref.shape[-1]
    energy, active = energy_ref[0], energy_ref[1]
    unit = jnp.where(
        iota((orbitals, orbitals), 0) == iota((orbitals, orbitals), 1), 1.0, 0.0
    )
    system = [
        jnp.concatenate(
            [
                energy * unit - onsite_ref[0, n] - sigma_ref[0, n],
                broadening * unit - onsite_ref[1, n] - sigma_ref[1, n],
            ],
            1,
        )
        for n in range(2)
    ]
    within = jnp.concatenate([hopping_ref[0, 0], hopping_ref[1, 0]], 1)
    beyond = jnp.concatenate([hopping_ref[0, 1], hopping_ref[1, 1]], 1) * active
    within_adjoint, beyond_adjoint = adjoint(within), adjoint(beyond)
    own_ref[0], own_ref[1] = system
    own_ref[2], own_ref[3] = within, within_adjoint
    own_ref[4], own_ref[5] = beyond, beyond_adjoint
    sides = (within, within_adjoint, beyond, beyond_adjoint)
    products, unused = eliminate(system[1], system[1], sides, sides)
    reduced_ref[0] = system[0] - products[0]
    reduced_ref[1] = products[3]
    reduced_ref[2] = -products[1]
    reduced_ref[3] = -products[2]


def solve_kernel(count, own_ref, *refs):
    others, green_ref = refs[:-1], refs[-1]
    even, odd = own_ref[0], own_ref[1]
    within, within_adjoint = own_ref[2], own_ref[3]
    blocks = {turn: others[turn - 1][0] for turn in range(1, count)}
    for turn in range(1, count - 1):
        blocks[turn + 1] = blocks[turn + 1] - others[turn - 1][1]
    blocks[0] = odd
    blocks[count] = even - others[count - 2][1]
    links = {turn: (others[turn - 1][2], others[turn - 1][3]) for turn in range(1, count)}
    links[0] = (-own_ref[4], -own_ref[5])
    stride = 1
    while stride < count:
        turns = list(range(stride, count, 2 * stride))
        last = len(turns) == 1
        for start in range(0, len(turns), 2):
            chosen = turns[start : start + 2]
            both = chosen if len(chosen) == 2 else chosen * 2
            sides = [links[t - stride] + links[t] for t in both]
            results = eliminate(blocks[both[0]], blocks[both[1]], sides[0], sides[1])
            for t, (left_left, left_right, right_left, right_right) in zip(chosen, results):
                blocks[t - stride] = blocks[t - stride] - left_left
                blocks[t + stride] = blocks[t + stride] - right_right
                if not last:
                    links[t - stride] = (-left_right, -right_left)
        stride *= 2
    even, odd = blocks[count], blocks[0]
    real, imag = invert_pair(even, odd)
    right_even, right_odd = pair_solve(real, imag, [within], [within_adjoint])
    odd_new = odd - matmul(within_adjoint, right_even)
    even_new = even - matmul(within, right_odd)
    real, imag = invert_pair(even_new, odd_new)
    rows = even.shape[0]
    green_ref[:rows], green_ref[rows:] = side_of_pair(real, imag)


def convolve_kernel(green_ref, screened_ref, out_ref, lag_ref):
    energies, rows, width = green_ref.shape
    lags = screened_ref.shape[1]
    half = width // 2
    for part in range(2):
        lag_ref[part, : lags - energies] = screened_ref[part, energies:]
        lag_ref[part, lags - energies : lags] = screened_ref[part, :energies]
    low = iota((energies, width), 1) < half
    for tile in range(rows // 2):
        place = pl.ds(tile * width, width)
        first, second = green_ref[:, 2 * tile, :], green_ref[:, 2 * tile + 1, :]
        real = jnp.where(low, first, swap_halves(second))
        imag = jnp.where(low, swap_halves(first), second)
        out_real = jnp.zeros((energies, width), jnp.float32)
        out_imag = jnp.zeros((energies, width), jnp.float32)
        for source in range(energies):
            window = pl.ds(lags - energies - source, energies)
            screen_real, screen_imag = lag_ref[0, window, place], lag_ref[1, window, place]
            a = jnp.broadcast_to(real[source : source + 1], (energies, width))
            b = jnp.broadcast_to(imag[source : source + 1], (energies, width))
            out_real = out_real + a * screen_real - b * screen_imag
            out_imag = out_imag + a * screen_imag + b * screen_real
        out_ref[0, :, place] = out_real
        out_ref[1, :, place] = out_imag


def local(onsite, hopping, sigma_prior, screened):
    blocks, orbitals = onsite.shape[1], onsite.shape[-1]
    space_count = lax.axis_size("space")
    energy_count = lax.axis_size("energy")
    if blocks != 2 or sigma_prior.shape[1] != 1 or space_count & (space_count - 1):
        raise ValueError("unsupported placement")
    width = 2 * orbitals
    side = jax.ShapeDtypeStruct((orbitals, width), jnp.float32)
    level = lax.axis_index("energy").astype(jnp.float32)
    energy = energy_low + (energy_high - energy_low) * (level + 0.5) / energy_count
    active = (lax.axis_index("space") < space_count - 1).astype(jnp.float32)
    whole = pl.BlockSpec(memory_space=pltpu.VMEM)
    own, reduced = pl.pallas_call(
        reduce_kernel,
        out_shape=(
            jax.ShapeDtypeStruct((6,) + side.shape, jnp.float32),
            jax.ShapeDtypeStruct((4,) + side.shape, jnp.float32),
        ),
        in_specs=[pl.BlockSpec(memory_space=pltpu.SMEM), whole, whole, whole],
        out_specs=(whole, whole),
    )(jnp.stack([energy, active]), onsite, hopping, sigma_prior.reshape(onsite.shape))
    others = [
        lax.ppermute(
            reduced,
            "space",
            [((r + turn) % space_count, r) for r in range(space_count)],
        )
        for turn in range(1, space_count)
    ]
    green = pl.pallas_call(
        functools.partial(solve_kernel, space_count),
        out_shape=jax.ShapeDtypeStruct((blocks * orbitals, width), jnp.float32),
        in_specs=[whole] * space_count,
        out_specs=whole,
    )(own, *others)
    pieces = green.reshape(energy_count, blocks * orbitals // energy_count, width)
    gathered = lax.all_to_all(pieces, "energy", split_axis=0, concat_axis=0, tiled=True)
    lag_count, entries = screened.shape[1:]
    return pl.pallas_call(
        convolve_kernel,
        out_shape=jax.ShapeDtypeStruct((2, energy_count, entries), jnp.float32),
        in_specs=[whole, whole],
        out_specs=whole,
        scratch_shapes=[pltpu.VMEM((2, lag_count + 1, entries), jnp.float32)],
    )(gathered, screened)


def solution(mesh):
    in_specs = (
        P(None, "space", None, None),
        P(None, "space", None, None),
        P(None, "energy", "space", None, None),
        P(None, None, ("space", "energy")),
    )
    out_specs = P(None, None, ("space", "energy"))
    return jax.shard_map(local, mesh=mesh, in_specs=in_specs, out_specs=out_specs, check_vma=False)
```

```python
import functools

import jax
import jax.numpy as jnp
from jax import lax
from jax.experimental import pallas as pl
from jax.experimental.pallas import tpu as pltpu
from jax.sharding import PartitionSpec as P

broadening = 0.25
energy_low = -3.0
energy_high = 3.0

PANEL = 8
SMALL = 2.0**-48


def iota(shape, dim):
    return lax.broadcasted_iota(jnp.int32, shape, dim)


def swap_halves(x):
    return pltpu.roll(x, x.shape[1] // 2, 1)


def low_half(x):
    return iota(x.shape, 1) < x.shape[1] // 2


def sublane_broadcast(x, row):
    return jnp.broadcast_to(x[row : row + 1, :], x.shape)


def complex_times(a, b):
    return a[0] * b[0] - a[1] * b[1], a[0] * b[1] + a[1] * b[0]


def minus(a, b):
    return a[0] - b[0], a[1] - b[1]


def tree_sum(terms):
    while len(terms) > 1:
        paired = [terms[n] + terms[n + 1] for n in range(0, len(terms) - 1, 2)]
        terms = paired + terms[len(paired) * 2 :]
    return terms[0]


def eliminate_panel(real, imag, panel):
    shape = real[0].shape
    half = shape[1] // 2
    lane, sub = iota(shape, 1) & (half - 1), iota(shape, 0)
    inside = (lane // PANEL) == panel
    unit = jnp.where((lane & (PANEL - 1)) == sub, 1.0, 0.0)
    places = [(iota(shape, 1) & half) + (panel * PANEL + c) for c in range(PANEL)]

    def column(x, c):
        return jnp.take_along_axis(x, places[c], axis=1, mode="promise_in_bounds")

    block = [
        (column(real[panel], c) * SMALL, column(imag[panel], c) * SMALL) for c in range(PANEL)
    ]
    rows = (jnp.where(inside, unit, real[panel]), jnp.where(inside, 0.0, imag[panel]))
    scale = (jnp.zeros(shape, jnp.float32), jnp.zeros(shape, jnp.float32))

    def spread(pair, row):
        return sublane_broadcast(pair[0], row), sublane_broadcast(pair[1], row)

    pivot = spread(block[0], 0)
    for step in range(PANEL):
        here = sub == step
        factor = 1.0 / (pivot[0] * pivot[0] + pivot[1] * pivot[1])
        recip = (pivot[0] * factor, -(pivot[1] * factor))
        if step < PANEL - 1:
            product = complex_times(spread(block[step], step + 1), spread(block[step + 1], step))
            pivot = minus(spread(block[step + 1], step + 1), complex_times(product, recip))
        rest = (jnp.where(here, 0.0, block[step][0]), jnp.where(here, 0.0, block[step][1]))
        multiple = complex_times(rest, recip)
        scale = (jnp.where(here, recip[0], scale[0]), jnp.where(here, recip[1], scale[1]))
        for c in range(step + 1, PANEL):
            block[c] = minus(block[c], complex_times(multiple, spread(block[c], step)))
        rows = minus(rows, complex_times(multiple, spread(rows, step)))
    rows = complex_times(rows, (scale[0] * SMALL, scale[1] * SMALL))
    spreads = [spread(rows, c) for c in range(PANEL)]
    others = [(panel + ahead) % len(real) for ahead in range(1, len(real))]
    columns = {group: [] for group in others}
    for c in range(PANEL):
        for group in others:
            columns[group].append((column(real[group], c), column(imag[group], c)))
    new_real, new_imag = list(real), list(imag)
    for group in others:
        terms = [complex_times(a, b) for a, b in zip(columns[group], spreads)]
        new_real[group] = jnp.where(inside, 0.0, real[group]) - tree_sum([t[0] for t in terms])
        new_imag[group] = jnp.where(inside, 0.0, imag[group]) - tree_sum([t[1] for t in terms])
    new_real[panel], new_imag[panel] = rows
    return new_real, new_imag


def invert_pair(first, second):
    low = low_half(first)
    real = jnp.where(low, first, swap_halves(second))
    imag = jnp.where(low, swap_halves(first), second)
    groups = first.shape[0] // PANEL
    real = [real[PANEL * g : PANEL * (g + 1)] for g in range(groups)]
    imag = [imag[PANEL * g : PANEL * (g + 1)] for g in range(groups)]
    for panel in range(groups):
        real, imag = eliminate_panel(real, imag, panel)
    return jnp.concatenate(real, 0), jnp.concatenate(imag, 0)


def side_of_pair(real, imag):
    low = low_half(real)
    return jnp.where(low, real, swap_halves(imag)), jnp.where(low, swap_halves(real), imag)


def times_i(x):
    turned = swap_halves(x)
    return jnp.where(low_half(x), -turned, turned)


def matmul(a, b):
    a_high, b_high = a.astype(jnp.bfloat16), b.astype(jnp.bfloat16)
    a_low = (a - a_high.astype(jnp.float32)).astype(jnp.bfloat16)
    b_low = (b - b_high.astype(jnp.float32)).astype(jnp.bfloat16)
    return jnp.dot(
        jnp.concatenate([a_high, a_high, a_low], 1),
        jnp.concatenate([b_high, b_low, b_high], 0),
        preferred_element_type=jnp.float32,
    )


def pair_solve(real, imag, right_first, right_second):
    low = low_half(real)
    left = jnp.concatenate(
        [
            jnp.concatenate([jnp.where(low, real, 0.0), jnp.where(low, imag, 0.0)], 1),
            jnp.concatenate([jnp.where(low, 0.0, real), jnp.where(low, 0.0, imag)], 1),
        ],
        0,
    )
    rows = real.shape[0]
    firsts, seconds = [], []
    for a, b in zip(right_first, right_second):
        stacked = jnp.concatenate([a, b], 0)
        turned = times_i(stacked)
        right = jnp.concatenate(
            [
                jnp.concatenate([stacked, turned], 1),
                jnp.concatenate([turned, -stacked], 1),
            ],
            0,
        )
        product = matmul(left, right)
        width = stacked.shape[1]
        firsts.append(jnp.concatenate([product[:rows, :width], product[:rows, width:]], 0))
        seconds.append(jnp.concatenate([product[rows:, :width], product[rows:, width:]], 0))
    return jnp.concatenate(firsts, 1), jnp.concatenate(seconds, 1)


def eliminate(block_first, block_second, sides_first, sides_second):
    real, imag = invert_pair(block_first, block_second)
    right_first, right_second = pair_solve(
        real,
        imag,
        [sides_first[1], sides_first[2]],
        [sides_second[1], sides_second[2]],
    )
    results = []
    for sides, right in ((sides_first, right_first), (sides_second, right_second)):
        rows, width = sides[0].shape
        out = matmul(jnp.concatenate([sides[0], sides[3]], 0), right)
        results.append(
            (out[:rows, :width], out[:rows, width:], out[rows:, :width], out[rows:, width:])
        )
    return results


def adjoint(x):
    half = x.shape[1] // 2
    turned = x.T
    return jnp.concatenate([turned[:half], -turned[half:]], 1)


def reduce_kernel(space_count, energy_count, onsite_ref, hopping_ref, sigma_ref, own_ref, reduced_ref):
    orbitals = onsite_ref.shape[-1]
    level = lax.axis_index("energy").astype(jnp.float32)
    energy = energy_low + (energy_high - energy_low) * (level + 0.5) / energy_count
    active = jnp.where(lax.axis_index("space") < space_count - 1, 1.0, 0.0)
    unit = jnp.where(
        iota((orbitals, orbitals), 0) == iota((orbitals, orbitals), 1), 1.0, 0.0
    )
    system = [
        jnp.concatenate(
            [
                energy * unit - onsite_ref[0, n] - sigma_ref[0, n],
                broadening * unit - onsite_ref[1, n] - sigma_ref[1, n],
            ],
            1,
        )
        for n in range(2)
    ]
    within = jnp.concatenate([hopping_ref[0, 0], hopping_ref[1, 0]], 1)
    beyond = jnp.concatenate([hopping_ref[0, 1], hopping_ref[1, 1]], 1) * active
    within_adjoint, beyond_adjoint = adjoint(within), adjoint(beyond)
    own_ref[0], own_ref[1] = system
    own_ref[2], own_ref[3] = within, within_adjoint
    own_ref[4], own_ref[5] = beyond, beyond_adjoint
    sides = (within, within_adjoint, beyond, beyond_adjoint)
    products, unused = eliminate(system[1], system[1], sides, sides)
    reduced_ref[0] = system[0] - products[0]
    reduced_ref[1] = products[3]
    reduced_ref[2] = -products[1]
    reduced_ref[3] = -products[2]


def solve_kernel(count, own_ref, *refs):
    flipped, green_ref = refs[:-1], refs[-1]
    place = lax.axis_index("space")

    def other(turn, part):
        flips = sorted({r ^ ((r + turn) % count) for r in range(count)})
        wanted = place ^ ((place + turn) & (count - 1))
        value = flipped[flips[0] - 1][part]
        for flip in flips[1:]:
            value = jnp.where(wanted == flip, flipped[flip - 1][part], value)
        return value

    even, odd = own_ref[0], own_ref[1]
    within, within_adjoint = own_ref[2], own_ref[3]
    blocks = {turn: other(turn, 0) for turn in range(1, count)}
    for turn in range(1, count - 1):
        blocks[turn + 1] = blocks[turn + 1] - other(turn, 1)
    blocks[0] = odd
    blocks[count] = even - other(count - 1, 1)
    links = {turn: (other(turn, 2), other(turn, 3)) for turn in range(1, count)}
    links[0] = (-own_ref[4], -own_ref[5])
    stride = 1
    while stride < count:
        turns = list(range(stride, count, 2 * stride))
        last = len(turns) == 1
        for start in range(0, len(turns), 2):
            chosen = turns[start : start + 2]
            both = chosen if len(chosen) == 2 else chosen * 2
            sides = [links[t - stride] + links[t] for t in both]
            results = eliminate(blocks[both[0]], blocks[both[1]], sides[0], sides[1])
            for t, (left_left, left_right, right_left, right_right) in zip(chosen, results):
                blocks[t - stride] = blocks[t - stride] - left_left
                blocks[t + stride] = blocks[t + stride] - right_right
                if not last:
                    links[t - stride] = (-left_right, -right_left)
        stride *= 2
    even, odd = blocks[count], blocks[0]
    real, imag = invert_pair(even, odd)
    right_even, right_odd = pair_solve(real, imag, [within], [within_adjoint])
    odd_new = odd - matmul(within_adjoint, right_even)
    even_new = even - matmul(within, right_odd)
    real, imag = invert_pair(even_new, odd_new)
    rows = even.shape[0]
    green_ref[:rows], green_ref[rows:] = side_of_pair(real, imag)


def window_kernel(screened_ref, window_ref, lag_ref):
    sources = window_ref.shape[1]
    lags = screened_ref.shape[1]
    for part in range(2):
        lag_ref[part, : lags - sources] = screened_ref[part, sources:]
        lag_ref[part, lags - sources : lags] = screened_ref[part, :sources]
        for source in range(sources):
            window_ref[part, source] = lag_ref[part, pl.ds(lags - sources - source, sources)]


def convolve_kernel(green_ref, window_ref, out_ref):
    energies, rows, width = green_ref.shape
    low = iota((energies, width), 1) < width // 2
    for tile in range(rows // 2):
        place = pl.ds(tile * width, width)
        first, second = green_ref[:, 2 * tile, :], green_ref[:, 2 * tile + 1, :]
        real = jnp.where(low, first, swap_halves(second))
        imag = jnp.where(low, swap_halves(first), second)
        terms = []
        for source in range(energies):
            green = (
                jnp.broadcast_to(real[source : source + 1], (energies, width)),
                jnp.broadcast_to(imag[source : source + 1], (energies, width)),
            )
            screen = (window_ref[0, source, :, place], window_ref[1, source, :, place])
            terms.append(complex_times(green, screen))
        out_ref[0, :, place] = tree_sum([t[0] for t in terms])
        out_ref[1, :, place] = tree_sum([t[1] for t in terms])


def in_vmem(x):
    return pltpu.with_memory_space_constraint(x, pltpu.VMEM)


def local(onsite, hopping, sigma_prior, screened):
    blocks, orbitals = onsite.shape[1], onsite.shape[-1]
    space_count = lax.axis_size("space")
    energy_count = lax.axis_size("energy")
    if blocks != 2 or sigma_prior.shape[1] != 1 or space_count & (space_count - 1):
        raise ValueError("unsupported placement")
    width = 2 * orbitals
    whole = pl.BlockSpec(memory_space=pltpu.VMEM)
    params = pltpu.CompilerParams(vmem_limit_bytes=24 * 2**20)
    own, reduced = pl.pallas_call(
        functools.partial(reduce_kernel, space_count, energy_count),
        out_shape=(
            pltpu.VMEM((6, orbitals, width), jnp.float32),
            pltpu.VMEM((4, orbitals, width), jnp.float32),
        ),
        compiler_params=params,
        in_specs=[whole] * 3,
        out_specs=(whole, whole),
    )(onsite, hopping, sigma_prior.reshape(onsite.shape))
    held = {0: reduced}
    bit = space_count // 2
    while bit:
        pairs = [(r, r ^ bit) for r in range(space_count)]
        held |= {flip ^ bit: lax.ppermute(held[flip], "space", pairs) for flip in list(held)}
        bit //= 2
    others = [in_vmem(held[flip]) for flip in range(1, space_count)]
    green = pl.pallas_call(
        functools.partial(solve_kernel, space_count),
        out_shape=pltpu.VMEM((blocks * orbitals, width), jnp.float32),
        compiler_params=params,
        in_specs=[whole] * space_count,
        out_specs=whole,
    )(in_vmem(own), *others)
    pieces = green.reshape(energy_count, blocks * orbitals // energy_count, width)
    gathered = lax.all_to_all(pieces, "energy", split_axis=0, concat_axis=0, tiled=True)
    lag_count, entries = screened.shape[1:]
    window = pl.pallas_call(
        window_kernel,
        out_shape=pltpu.VMEM((2, energy_count, energy_count, entries), jnp.float32),
        compiler_params=params,
        in_specs=[whole],
        out_specs=whole,
        scratch_shapes=[pltpu.VMEM((2, lag_count + 1, entries), jnp.float32)],
        cost_estimate=pl.CostEstimate(
            flops=0, transcendentals=0, bytes_accessed=16 * energy_count**2 * entries
        ),
    )(screened)
    return pl.pallas_call(
        convolve_kernel,
        out_shape=jax.ShapeDtypeStruct((2, energy_count, entries), jnp.float32),
        compiler_params=params,
        in_specs=[whole, whole],
        out_specs=whole,
    )(in_vmem(gathered), in_vmem(window))


def solution(mesh):
    in_specs = (
        P(None, "space", None, None),
        P(None, "space", None, None),
        P(None, "energy", "space", None, None),
        P(None, None, ("space", "energy")),
    )
    out_specs = P(None, None, ("space", "energy"))
    return jax.shard_map(local, mesh=mesh, in_specs=in_specs, out_specs=out_specs, check_vma=False)
```

```python
import functools

import jax
import jax.numpy as jnp
from jax import lax
from jax.experimental import pallas as pl
from jax.experimental.pallas import tpu as pltpu
from jax.sharding import PartitionSpec as P

broadening = 0.25
energy_low = -3.0
energy_high = 3.0

PANEL = 8
SMALL = 2.0**-48


def iota(shape, dim):
    return lax.broadcasted_iota(jnp.int32, shape, dim)


def swap_halves(x):
    return pltpu.roll(x, x.shape[1] // 2, 1)


def low_half(x):
    return iota(x.shape, 1) < x.shape[1] // 2


def sublane_broadcast(x, row):
    return jnp.broadcast_to(x[row : row + 1, :], x.shape)


def complex_times(a, b):
    return a[0] * b[0] - a[1] * b[1], a[0] * b[1] + a[1] * b[0]


def minus(a, b):
    return a[0] - b[0], a[1] - b[1]


def tree_sum(terms):
    while len(terms) > 1:
        paired = [terms[n] + terms[n + 1] for n in range(0, len(terms) - 1, 2)]
        terms = paired + terms[len(paired) * 2 :]
    return terms[0]


def invert_groups(real, imag):
    real, imag = list(real), list(imag)
    count, shape = len(real), real[0].shape
    half = shape[1] // 2
    lane, sub = iota(shape, 1) & (half - 1), iota(shape, 0)
    unit = jnp.where((lane & (PANEL - 1)) == sub, 1.0, 0.0)

    def columns(panel, groups):
        found = {group: [] for group in groups}
        for c in range(PANEL):
            place = (iota(shape, 1) & half) + (panel * PANEL + c)
            for group in groups:
                found[group].append(
                    tuple(
                        jnp.take_along_axis(x, place, axis=1, mode="promise_in_bounds")
                        for x in (real[group], imag[group])
                    )
                )
        return found

    def spread(pair, row):
        return sublane_broadcast(pair[0], row), sublane_broadcast(pair[1], row)

    block = columns(0, [0])[0]
    for panel in range(count):
        following = (panel + 1) % count
        rest = [group for group in range(count) if group not in (panel, following)]
        inside = (lane // PANEL) == panel
        column = columns(panel, [following])
        column |= columns(panel, rest)
        block = [(a * SMALL, b * SMALL) for a, b in block]
        rows = (jnp.where(inside, unit, real[panel]), jnp.where(inside, 0.0, imag[panel]))
        scale = (jnp.zeros(shape, jnp.float32), jnp.zeros(shape, jnp.float32))
        pivot = spread(block[0], 0)
        for step in range(PANEL):
            here = sub == step
            factor = 1.0 / (pivot[0] * pivot[0] + pivot[1] * pivot[1])
            recip = (pivot[0] * factor, -(pivot[1] * factor))
            if step < PANEL - 1:
                product = complex_times(
                    spread(block[step], step + 1), spread(block[step + 1], step)
                )
                pivot = minus(spread(block[step + 1], step + 1), complex_times(product, recip))
            outer = (jnp.where(here, 0.0, block[step][0]), jnp.where(here, 0.0, block[step][1]))
            multiple = complex_times(outer, recip)
            scale = (jnp.where(here, recip[0], scale[0]), jnp.where(here, recip[1], scale[1]))
            for c in range(step + 1, PANEL):
                block[c] = minus(block[c], complex_times(multiple, spread(block[c], step)))
            rows = minus(rows, complex_times(multiple, spread(rows, step)))
        rows = complex_times(rows, (scale[0] * SMALL, scale[1] * SMALL))
        spreads = [spread(rows, c) for c in range(PANEL)]
        real[panel], imag[panel] = rows
        for group in [following] + rest:
            terms = [complex_times(a, b) for a, b in zip(column[group], spreads)]
            real[group] = jnp.where(inside, 0.0, real[group]) - tree_sum([t[0] for t in terms])
            imag[group] = jnp.where(inside, 0.0, imag[group]) - tree_sum([t[1] for t in terms])
            if group == following and panel < count - 1:
                block = columns(following, [following])[following]
    return real, imag


def invert_pair(first, second):
    low = low_half(first)
    real = jnp.where(low, first, swap_halves(second))
    imag = jnp.where(low, swap_halves(first), second)
    groups = first.shape[0] // PANEL
    real = [real[PANEL * g : PANEL * (g + 1)] for g in range(groups)]
    imag = [imag[PANEL * g : PANEL * (g + 1)] for g in range(groups)]
    real, imag = invert_groups(real, imag)
    return jnp.concatenate(real, 0), jnp.concatenate(imag, 0)


def side_of_pair(real, imag):
    low = low_half(real)
    return jnp.where(low, real, swap_halves(imag)), jnp.where(low, swap_halves(real), imag)


def times_i(x):
    turned = swap_halves(x)
    return jnp.where(low_half(x), -turned, turned)


def matmul(a, b):
    a_high, b_high = a.astype(jnp.bfloat16), b.astype(jnp.bfloat16)
    a_low = (a - a_high.astype(jnp.float32)).astype(jnp.bfloat16)
    b_low = (b - b_high.astype(jnp.float32)).astype(jnp.bfloat16)
    return jnp.dot(
        jnp.concatenate([a_high, a_high, a_low], 1),
        jnp.concatenate([b_high, b_low, b_high], 0),
        preferred_element_type=jnp.float32,
    )


def pair_solve(real, imag, right_first, right_second):
    low = low_half(real)
    left = jnp.concatenate(
        [
            jnp.concatenate([jnp.where(low, real, 0.0), jnp.where(low, imag, 0.0)], 1),
            jnp.concatenate([jnp.where(low, 0.0, real), jnp.where(low, 0.0, imag)], 1),
        ],
        0,
    )
    rows = real.shape[0]
    firsts, seconds = [], []
    for a, b in zip(right_first, right_second):
        stacked = jnp.concatenate([a, b], 0)
        turned = times_i(stacked)
        right = jnp.concatenate(
            [
                jnp.concatenate([stacked, turned], 1),
                jnp.concatenate([turned, -stacked], 1),
            ],
            0,
        )
        product = matmul(left, right)
        width = stacked.shape[1]
        firsts.append(jnp.concatenate([product[:rows, :width], product[:rows, width:]], 0))
        seconds.append(jnp.concatenate([product[rows:, :width], product[rows:, width:]], 0))
    return jnp.concatenate(firsts, 1), jnp.concatenate(seconds, 1)


def eliminate(block_first, block_second, sides_first, sides_second):
    real, imag = invert_pair(block_first, block_second)
    right_first, right_second = pair_solve(
        real,
        imag,
        [sides_first[1], sides_first[2]],
        [sides_second[1], sides_second[2]],
    )
    results = []
    for sides, right in ((sides_first, right_first), (sides_second, right_second)):
        rows, width = sides[0].shape
        out = matmul(jnp.concatenate([sides[0], sides[3]], 0), right)
        results.append(
            (out[:rows, :width], out[:rows, width:], out[rows:, :width], out[rows:, width:])
        )
    return results


def adjoint(x):
    half = x.shape[1] // 2
    turned = x.T
    return jnp.concatenate([turned[:half], -turned[half:]], 1)


def reduce_kernel(space_count, energy_count, onsite_ref, hopping_ref, sigma_ref, own_ref, reduced_ref):
    orbitals = onsite_ref.shape[-1]
    level = lax.axis_index("energy").astype(jnp.float32)
    energy = energy_low + (energy_high - energy_low) * (level + 0.5) / energy_count
    active = jnp.where(lax.axis_index("space") < space_count - 1, 1.0, 0.0)
    unit = jnp.where(
        iota((orbitals, orbitals), 0) == iota((orbitals, orbitals), 1), 1.0, 0.0
    )
    system = [
        jnp.concatenate(
            [
                energy * unit - onsite_ref[0, n] - sigma_ref[0, n],
                broadening * unit - onsite_ref[1, n] - sigma_ref[1, n],
            ],
            1,
        )
        for n in range(2)
    ]
    within = jnp.concatenate([hopping_ref[0, 0], hopping_ref[1, 0]], 1)
    beyond = jnp.concatenate([hopping_ref[0, 1], hopping_ref[1, 1]], 1) * active
    within_adjoint, beyond_adjoint = adjoint(within), adjoint(beyond)
    own_ref[0], own_ref[1] = system
    own_ref[2], own_ref[3] = within, within_adjoint
    own_ref[4], own_ref[5] = beyond, beyond_adjoint
    sides = (within, within_adjoint, beyond, beyond_adjoint)
    products, unused = eliminate(system[1], system[1], sides, sides)
    reduced_ref[0] = system[0] - products[0]
    reduced_ref[1] = products[3]
    reduced_ref[2] = -products[1]
    reduced_ref[3] = -products[2]


def solve_kernel(count, own_ref, *refs):
    flipped, (keep_ref, give_ref, green_ref) = refs[:-3], refs[-3:]
    place = lax.axis_index("space")

    def other(turn, part):
        flips = sorted({r ^ ((r + turn) % count) for r in range(count)})
        wanted = place ^ ((place + turn) & (count - 1))
        value = flipped[flips[0] - 1][part]
        for flip in flips[1:]:
            value = jnp.where(wanted == flip, flipped[flip - 1][part], value)
        return value

    even, odd = own_ref[0], own_ref[1]
    within, within_adjoint = own_ref[2], own_ref[3]
    blocks = {turn: other(turn, 0) for turn in range(1, count)}
    for turn in range(1, count - 1):
        blocks[turn + 1] = blocks[turn + 1] - other(turn, 1)
    blocks[0] = odd
    blocks[count] = even - other(count - 1, 1)
    links = {turn: (other(turn, 2), other(turn, 3)) for turn in range(1, count)}
    links[0] = (-own_ref[4], -own_ref[5])
    stride = 1
    while stride < count:
        turns = list(range(stride, count, 2 * stride))
        last = len(turns) == 1
        for start in range(0, len(turns), 2):
            chosen = turns[start : start + 2]
            both = chosen if len(chosen) == 2 else chosen * 2
            sides = [links[t - stride] + links[t] for t in both]
            results = eliminate(blocks[both[0]], blocks[both[1]], sides[0], sides[1])
            for t, (left_left, left_right, right_left, right_right) in zip(chosen, results):
                blocks[t - stride] = blocks[t - stride] - left_left
                blocks[t + stride] = blocks[t + stride] - right_right
                if not last:
                    links[t - stride] = (-left_right, -right_left)
        stride *= 2
    even, odd = blocks[count], blocks[0]
    real, imag = invert_pair(even, odd)
    right_even, right_odd = pair_solve(real, imag, [within], [within_adjoint])
    odd_new = odd - matmul(within_adjoint, right_even)
    even_new = even - matmul(within, right_odd)
    real, imag = invert_pair(even_new, odd_new)
    pieces, rows = green_ref.shape[:2]
    first, second = side_of_pair(real, imag)
    for piece in range(pieces // 2):
        green_ref[piece] = first[piece * rows : (piece + 1) * rows]
        green_ref[pieces // 2 + piece] = second[piece * rows : (piece + 1) * rows]
    rank = lax.axis_index("energy")
    for slot in range(pieces // 2):
        keep_ref[slot] = green_ref[rank ^ (2 * slot)]
        give_ref[slot] = green_ref[rank ^ (2 * slot + 1)]


def window_kernel(screened_ref, window_ref, lag_ref):
    sources = window_ref.shape[1]
    lags = screened_ref.shape[1]
    for part in range(2):
        lag_ref[part, : lags - sources] = screened_ref[part, sources:]
        lag_ref[part, lags - sources : lags] = screened_ref[part, :sources]
        for source in range(sources):
            window_ref[part, source] = lag_ref[part, pl.ds(lags - sources - source, sources)]


def exchange_kernel(dests, kept_ref, got_ref, keep_ref, give_ref):
    held = kept_ref.shape[0]
    for source in range(2 * held // dests):
        ref, base = (kept_ref, 0) if source * dests < held else (got_ref, held)
        for dest in range(dests):
            to_ref = give_ref if dest % 2 else keep_ref
            to_ref[(source * dests + dest) // 2] = ref[source * dests + dest - base]


def convolve_kernel(kept_ref, got_ref, window_ref, out_ref):
    half, rows, width = kept_ref.shape
    energies = 2 * half
    low = iota((half, width), 1) < width // 2
    rank = lax.axis_index("energy")
    for tile in range(rows // 2):
        place = pl.ds(tile * width, width)
        terms = []
        for part, ref in enumerate((kept_ref, got_ref)):
            first, second = ref[:, 2 * tile, :], ref[:, 2 * tile + 1, :]
            real = jnp.where(low, first, swap_halves(second))
            imag = jnp.where(low, swap_halves(first), second)
            for n in range(half):
                source = rank ^ (part * half + n)
                green = (
                    jnp.broadcast_to(real[n : n + 1], (energies, width)),
                    jnp.broadcast_to(imag[n : n + 1], (energies, width)),
                )
                screen = (window_ref[0, source, :, place], window_ref[1, source, :, place])
                terms.append(complex_times(green, screen))
        out_ref[0, :, place] = tree_sum([t[0] for t in terms])
        out_ref[1, :, place] = tree_sum([t[1] for t in terms])


def in_vmem(x):
    return pltpu.with_memory_space_constraint(x, pltpu.VMEM)


def local(onsite, hopping, sigma_prior, screened):
    blocks, orbitals = onsite.shape[1], onsite.shape[-1]
    space_count = lax.axis_size("space")
    energy_count = lax.axis_size("energy")
    if blocks != 2 or sigma_prior.shape[1] != 1 or space_count & (space_count - 1):
        raise ValueError("unsupported placement")
    width = 2 * orbitals
    whole = pl.BlockSpec(memory_space=pltpu.VMEM)
    params = pltpu.CompilerParams(vmem_limit_bytes=24 * 2**20)
    own, reduced = pl.pallas_call(
        functools.partial(reduce_kernel, space_count, energy_count),
        out_shape=(
            pltpu.VMEM((6, orbitals, width), jnp.float32),
            pltpu.VMEM((4, orbitals, width), jnp.float32),
        ),
        in_specs=[whole] * 3,
        out_specs=(whole, whole),
    )(onsite, hopping, sigma_prior.reshape(onsite.shape))
    held = {0: reduced}
    bit = space_count // 2
    while bit:
        pairs = [(r, r ^ bit) for r in range(space_count)]
        held |= {flip ^ bit: lax.ppermute(held[flip], "space", pairs) for flip in list(held)}
        bit //= 2
    others = [in_vmem(held[flip]) for flip in range(1, space_count)]
    piece = (blocks * orbitals // energy_count, width)
    halves = (pltpu.VMEM((energy_count // 2,) + piece, jnp.float32),) * 2
    keep, give = pl.pallas_call(
        functools.partial(solve_kernel, space_count),
        out_shape=halves,
        compiler_params=params,
        in_specs=[whole] * space_count,
        out_specs=(whole, whole),
        scratch_shapes=[pltpu.VMEM((energy_count,) + piece, jnp.float32)],
    )(in_vmem(own), *others)
    bit = 1
    while True:
        pairs = [(r, r ^ bit) for r in range(energy_count)]
        got = lax.ppermute(give, "energy", pairs)
        bit *= 2
        if bit == energy_count:
            break
        keep, give = pl.pallas_call(
            functools.partial(exchange_kernel, energy_count // bit),
            out_shape=halves,
            compiler_params=params,
            in_specs=[whole, whole],
            out_specs=(whole, whole),
        )(in_vmem(keep), in_vmem(got))
    lag_count, entries = screened.shape[1:]
    window = pl.pallas_call(
        window_kernel,
        out_shape=pltpu.VMEM((2, energy_count, energy_count, entries), jnp.float32),
        compiler_params=params,
        in_specs=[whole],
        out_specs=whole,
        scratch_shapes=[pltpu.VMEM((2, lag_count + 1, entries), jnp.float32)],
        cost_estimate=pl.CostEstimate(
            flops=0, transcendentals=0, bytes_accessed=16 * energy_count**2 * entries
        ),
    )(screened)
    return pl.pallas_call(
        convolve_kernel,
        out_shape=jax.ShapeDtypeStruct((2, energy_count, entries), jnp.float32),
        compiler_params=params,
        in_specs=[whole, whole, whole],
        out_specs=whole,
    )(in_vmem(keep), in_vmem(got), in_vmem(window))


def solution(mesh):
    in_specs = (
        P(None, "space", None, None),
        P(None, "space", None, None),
        P(None, "energy", "space", None, None),
        P(None, None, ("space", "energy")),
    )
    out_specs = P(None, None, ("space", "energy"))
    return jax.shard_map(local, mesh=mesh, in_specs=in_specs, out_specs=out_specs, check_vma=False)
```

```python
import functools

import jax
import jax.numpy as jnp
from jax import lax
from jax.experimental import pallas as pl
from jax.experimental.pallas import tpu as pltpu
from jax.sharding import PartitionSpec as P

broadening = 0.25
energy_low = -3.0
energy_high = 3.0

PANEL = 8
SMALL = 2.0**-48


def iota(shape, dim):
    return lax.broadcasted_iota(jnp.int32, shape, dim)


def swap_halves(x):
    return pltpu.roll(x, x.shape[1] // 2, 1)


def low_half(x):
    return iota(x.shape, 1) < x.shape[1] // 2


def sublane_broadcast(x, row):
    return jnp.broadcast_to(x[row : row + 1, :], x.shape)


def complex_times(a, b):
    return a[0] * b[0] - a[1] * b[1], a[0] * b[1] + a[1] * b[0]


def minus(a, b):
    return a[0] - b[0], a[1] - b[1]


def tree_sum(terms):
    while len(terms) > 1:
        paired = [terms[n] + terms[n + 1] for n in range(0, len(terms) - 1, 2)]
        terms = paired + terms[len(paired) * 2 :]
    return terms[0]


def invert_groups(real, imag, paired):
    real, imag = list(real), list(imag)
    count, shape = len(real), real[0].shape
    half = shape[1] // 2
    lane, sub = iota(shape, 1), iota(shape, 0)
    if paired:
        lane = lane & (half - 1)
    unit = jnp.where((lane & (PANEL - 1)) == sub, 1.0, 0.0)

    def columns(panel, groups):
        found = {group: [] for group in groups}
        for c in range(panel * PANEL, panel * PANEL + PANEL):
            place = (iota(shape, 1) & half) + c
            for group in groups:
                found[group].append(
                    tuple(
                        jnp.take_along_axis(x, place, axis=1, mode="promise_in_bounds")
                        if paired
                        else jnp.broadcast_to(x[:, c : c + 1], shape)
                        for x in (real[group], imag[group])
                    )
                )
        return found

    def spread(pair, row):
        return sublane_broadcast(pair[0], row), sublane_broadcast(pair[1], row)

    block = columns(0, [0])[0]
    for panel in range(count):
        following = (panel + 1) % count
        rest = [group for group in range(count) if group not in (panel, following)]
        inside = (lane // PANEL) == panel
        column = columns(panel, [following])
        column |= columns(panel, rest)
        block = [(a * SMALL, b * SMALL) for a, b in block]
        rows = (jnp.where(inside, unit, real[panel]), jnp.where(inside, 0.0, imag[panel]))
        scale = (jnp.zeros(shape, jnp.float32), jnp.zeros(shape, jnp.float32))
        pivot = spread(block[0], 0)
        for step in range(PANEL):
            here = sub == step
            factor = 1.0 / (pivot[0] * pivot[0] + pivot[1] * pivot[1])
            recip = (pivot[0] * factor, -(pivot[1] * factor))
            if step < PANEL - 1:
                product = complex_times(
                    spread(block[step], step + 1), spread(block[step + 1], step)
                )
                pivot = minus(spread(block[step + 1], step + 1), complex_times(product, recip))
            outer = (jnp.where(here, 0.0, block[step][0]), jnp.where(here, 0.0, block[step][1]))
            multiple = complex_times(outer, recip)
            scale = (jnp.where(here, recip[0], scale[0]), jnp.where(here, recip[1], scale[1]))
            for c in range(step + 1, PANEL):
                block[c] = minus(block[c], complex_times(multiple, spread(block[c], step)))
            rows = minus(rows, complex_times(multiple, spread(rows, step)))
        rows = complex_times(rows, (scale[0] * SMALL, scale[1] * SMALL))
        spreads = [spread(rows, c) for c in range(PANEL)]
        real[panel], imag[panel] = rows
        for group in [following] + rest:
            terms = [complex_times(a, b) for a, b in zip(column[group], spreads)]
            real[group] = jnp.where(inside, 0.0, real[group]) - tree_sum([t[0] for t in terms])
            imag[group] = jnp.where(inside, 0.0, imag[group]) - tree_sum([t[1] for t in terms])
            if group == following and panel < count - 1:
                block = columns(following, [following])[following]
    return real, imag


def invert_pair(first, second, paired=True):
    low = low_half(first)
    real = jnp.where(low, first, swap_halves(second))
    imag = jnp.where(low, swap_halves(first), second)
    groups = first.shape[0] // PANEL
    real = [real[PANEL * g : PANEL * (g + 1)] for g in range(groups)]
    imag = [imag[PANEL * g : PANEL * (g + 1)] for g in range(groups)]
    real, imag = invert_groups(real, imag, paired)
    return jnp.concatenate(real, 0), jnp.concatenate(imag, 0)


def side_of_pair(real, imag):
    low = low_half(real)
    return jnp.where(low, real, swap_halves(imag)), jnp.where(low, swap_halves(real), imag)


def times_i(x):
    turned = swap_halves(x)
    return jnp.where(low_half(x), -turned, turned)


def matmul(a, b):
    a_high, b_high = a.astype(jnp.bfloat16), b.astype(jnp.bfloat16)
    a_low = (a - a_high.astype(jnp.float32)).astype(jnp.bfloat16)
    b_low = (b - b_high.astype(jnp.float32)).astype(jnp.bfloat16)
    return jnp.dot(
        jnp.concatenate([a_high, a_high, a_low], 1),
        jnp.concatenate([b_high, b_low, b_high], 0),
        preferred_element_type=jnp.float32,
    )


def pair_solve(real, imag, right_first, right_second):
    low = low_half(real)
    left = jnp.concatenate(
        [
            jnp.concatenate([jnp.where(low, real, 0.0), jnp.where(low, imag, 0.0)], 1),
            jnp.concatenate([jnp.where(low, 0.0, real), jnp.where(low, 0.0, imag)], 1),
        ],
        0,
    )
    rows = real.shape[0]
    firsts, seconds = [], []
    for a, b in zip(right_first, right_second):
        stacked = jnp.concatenate([a, b], 0)
        turned = times_i(stacked)
        right = jnp.concatenate(
            [
                jnp.concatenate([stacked, turned], 1),
                jnp.concatenate([turned, -stacked], 1),
            ],
            0,
        )
        product = matmul(left, right)
        width = stacked.shape[1]
        firsts.append(jnp.concatenate([product[:rows, :width], product[:rows, width:]], 0))
        seconds.append(jnp.concatenate([product[rows:, :width], product[rows:, width:]], 0))
    return jnp.concatenate(firsts, 1), jnp.concatenate(seconds, 1)


def eliminate(block_first, block_second, sides_first, sides_second):
    real, imag = invert_pair(block_first, block_second)
    right_first, right_second = pair_solve(
        real,
        imag,
        [sides_first[1], sides_first[2]],
        [sides_second[1], sides_second[2]],
    )
    results = []
    for sides, right in ((sides_first, right_first), (sides_second, right_second)):
        rows, width = sides[0].shape
        out = matmul(jnp.concatenate([sides[0], sides[3]], 0), right)
        results.append(
            (out[:rows, :width], out[:rows, width:], out[rows:, :width], out[rows:, width:])
        )
    return results


def eliminate_one(block, sides):
    real, imag = invert_pair(block, sides[1], False)
    inverse, from_left = side_of_pair(real, imag)
    turned = times_i(sides[2])
    rows, width = block.shape
    from_right = matmul(
        inverse,
        jnp.concatenate(
            [jnp.concatenate([sides[2], turned], 1), jnp.concatenate([turned, -sides[2]], 1)], 0
        ),
    )
    right = jnp.concatenate(
        [
            jnp.concatenate([from_left, times_i(from_left)], 0),
            jnp.concatenate([from_right[:, :width], from_right[:, width:]], 0),
        ],
        1,
    )
    out = matmul(jnp.concatenate([sides[0], sides[3]], 0), right)
    return out[:rows, :width], out[:rows, width:], out[rows:, :width], out[rows:, width:]


def adjoint(x):
    half = x.shape[1] // 2
    turned = x.T
    return jnp.concatenate([turned[:half], -turned[half:]], 1)


def reduce_kernel(space_count, energy_count, onsite_ref, hopping_ref, sigma_ref, own_ref, reduced_ref):
    orbitals = onsite_ref.shape[-1]
    level = lax.axis_index("energy").astype(jnp.float32)
    energy = energy_low + (energy_high - energy_low) * (level + 0.5) / energy_count
    active = jnp.where(lax.axis_index("space") < space_count - 1, 1.0, 0.0)
    unit = jnp.where(
        iota((orbitals, orbitals), 0) == iota((orbitals, orbitals), 1), 1.0, 0.0
    )
    system = [
        jnp.concatenate(
            [
                energy * unit - onsite_ref[0, n] - sigma_ref[0, n],
                broadening * unit - onsite_ref[1, n] - sigma_ref[1, n],
            ],
            1,
        )
        for n in range(2)
    ]
    within = jnp.concatenate([hopping_ref[0, 0], hopping_ref[1, 0]], 1)
    beyond = jnp.concatenate([hopping_ref[0, 1], hopping_ref[1, 1]], 1) * active
    within_adjoint, beyond_adjoint = adjoint(within), adjoint(beyond)
    own_ref[0], own_ref[1] = system
    own_ref[2], own_ref[3] = within, within_adjoint
    own_ref[4], own_ref[5] = beyond, beyond_adjoint
    sides = (within, within_adjoint, beyond, beyond_adjoint)
    products = eliminate_one(system[1], sides)
    reduced_ref[0] = system[0] - products[0]
    reduced_ref[1] = products[3]
    reduced_ref[2] = -products[1]
    reduced_ref[3] = -products[2]


def solve_kernel(count, own_ref, *refs):
    flipped, (keep_ref, give_ref, green_ref) = refs[:-3], refs[-3:]
    place = lax.axis_index("space")

    def other(turn, part):
        flips = sorted({r ^ ((r + turn) % count) for r in range(count)})
        wanted = place ^ ((place + turn) & (count - 1))
        value = flipped[flips[0] - 1][part]
        for flip in flips[1:]:
            value = jnp.where(wanted == flip, flipped[flip - 1][part], value)
        return value

    even, odd = own_ref[0], own_ref[1]
    within, within_adjoint = own_ref[2], own_ref[3]
    blocks = {turn: other(turn, 0) for turn in range(1, count)}
    for turn in range(1, count - 1):
        blocks[turn + 1] = blocks[turn + 1] - other(turn, 1)
    blocks[0] = odd
    blocks[count] = even - other(count - 1, 1)
    links = {turn: (other(turn, 2), other(turn, 3)) for turn in range(1, count)}
    links[0] = (-own_ref[4], -own_ref[5])
    stride = 1
    while stride < count:
        turns = list(range(stride, count, 2 * stride))
        last = len(turns) == 1
        for start in range(0, len(turns), 2):
            chosen = turns[start : start + 2]
            sides = [links[t - stride] + links[t] for t in chosen]
            if len(chosen) == 1:
                results = [eliminate_one(blocks[chosen[0]], sides[0])]
            else:
                results = eliminate(blocks[chosen[0]], blocks[chosen[1]], sides[0], sides[1])
            for t, (left_left, left_right, right_left, right_right) in zip(chosen, results):
                blocks[t - stride] = blocks[t - stride] - left_left
                blocks[t + stride] = blocks[t + stride] - right_right
                if not last:
                    links[t - stride] = (-left_right, -right_left)
        stride *= 2
    even, odd = blocks[count], blocks[0]
    real, imag = invert_pair(even, odd)
    right_even, right_odd = pair_solve(real, imag, [within], [within_adjoint])
    odd_new = odd - matmul(within_adjoint, right_even)
    even_new = even - matmul(within, right_odd)
    real, imag = invert_pair(even_new, odd_new)
    pieces, rows = green_ref.shape[:2]
    first, second = side_of_pair(real, imag)
    for piece in range(pieces // 2):
        green_ref[piece] = first[piece * rows : (piece + 1) * rows]
        green_ref[pieces // 2 + piece] = second[piece * rows : (piece + 1) * rows]
    rank = lax.axis_index("energy")
    for slot in range(pieces // 2):
        keep_ref[slot] = green_ref[rank ^ (2 * slot)]
        give_ref[slot] = green_ref[rank ^ (2 * slot + 1)]


def window_kernel(screened_ref, window_ref, lag_ref):
    sources = window_ref.shape[1]
    lags = screened_ref.shape[1]
    for part in range(2):
        lag_ref[part, : lags - sources] = screened_ref[part, sources:]
        lag_ref[part, lags - sources : lags] = screened_ref[part, :sources]
        for source in range(sources):
            window_ref[part, source] = lag_ref[part, pl.ds(lags - sources - source, sources)]


def exchange_kernel(dests, kept_ref, got_ref, keep_ref, give_ref):
    held = kept_ref.shape[0]
    for source in range(2 * held // dests):
        ref, base = (kept_ref, 0) if source * dests < held else (got_ref, held)
        for dest in range(dests):
            to_ref = give_ref if dest % 2 else keep_ref
            to_ref[(source * dests + dest) // 2] = ref[source * dests + dest - base]


def convolve_kernel(kept_ref, got_ref, window_ref, out_ref):
    half, rows, width = kept_ref.shape
    energies = 2 * half
    low = iota((half, width), 1) < width // 2
    rank = lax.axis_index("energy")
    for tile in range(rows // 2):
        place = pl.ds(tile * width, width)
        terms = []
        for part, ref in enumerate((kept_ref, got_ref)):
            first, second = ref[:, 2 * tile, :], ref[:, 2 * tile + 1, :]
            real = jnp.where(low, first, swap_halves(second))
            imag = jnp.where(low, swap_halves(first), second)
            for n in range(half):
                source = rank ^ (part * half + n)
                green = (
                    jnp.broadcast_to(real[n : n + 1], (energies, width)),
                    jnp.broadcast_to(imag[n : n + 1], (energies, width)),
                )
                screen = (window_ref[0, source, :, place], window_ref[1, source, :, place])
                terms.append(complex_times(green, screen))
        out_ref[0, :, place] = tree_sum([t[0] for t in terms])
        out_ref[1, :, place] = tree_sum([t[1] for t in terms])


def in_vmem(x):
    return pltpu.with_memory_space_constraint(x, pltpu.VMEM)


def local(onsite, hopping, sigma_prior, screened):
    blocks, orbitals = onsite.shape[1], onsite.shape[-1]
    space_count = lax.axis_size("space")
    energy_count = lax.axis_size("energy")
    if blocks != 2 or sigma_prior.shape[1] != 1 or space_count & (space_count - 1):
        raise ValueError("unsupported placement")
    width = 2 * orbitals
    whole = pl.BlockSpec(memory_space=pltpu.VMEM)
    params = pltpu.CompilerParams(vmem_limit_bytes=24 * 2**20)
    own, reduced = pl.pallas_call(
        functools.partial(reduce_kernel, space_count, energy_count),
        out_shape=(
            pltpu.VMEM((6, orbitals, width), jnp.float32),
            pltpu.VMEM((4, orbitals, width), jnp.float32),
        ),
        in_specs=[whole] * 3,
        out_specs=(whole, whole),
    )(onsite, hopping, sigma_prior.reshape(onsite.shape))
    held = {0: reduced}
    bit = space_count // 2
    while bit:
        pairs = [(r, r ^ bit) for r in range(space_count)]
        held |= {flip ^ bit: lax.ppermute(held[flip], "space", pairs) for flip in list(held)}
        bit //= 2
    others = [in_vmem(held[flip]) for flip in range(1, space_count)]
    piece = (blocks * orbitals // energy_count, width)
    halves = (pltpu.VMEM((energy_count // 2,) + piece, jnp.float32),) * 2
    keep, give = pl.pallas_call(
        functools.partial(solve_kernel, space_count),
        out_shape=halves,
        compiler_params=params,
        in_specs=[whole] * space_count,
        out_specs=(whole, whole),
        scratch_shapes=[pltpu.VMEM((energy_count,) + piece, jnp.float32)],
    )(in_vmem(own), *others)
    bit = 1
    while True:
        pairs = [(r, r ^ bit) for r in range(energy_count)]
        got = lax.ppermute(give, "energy", pairs)
        bit *= 2
        if bit == energy_count:
            break
        keep, give = pl.pallas_call(
            functools.partial(exchange_kernel, energy_count // bit),
            out_shape=halves,
            compiler_params=params,
            in_specs=[whole, whole],
            out_specs=(whole, whole),
        )(in_vmem(keep), in_vmem(got))
    lag_count, entries = screened.shape[1:]
    window = pl.pallas_call(
        window_kernel,
        out_shape=pltpu.VMEM((2, energy_count, energy_count, entries), jnp.float32),
        compiler_params=params,
        in_specs=[whole],
        out_specs=whole,
        scratch_shapes=[pltpu.VMEM((2, lag_count + 1, entries), jnp.float32)],
        cost_estimate=pl.CostEstimate(
            flops=0, transcendentals=0, bytes_accessed=16 * energy_count**2 * entries
        ),
    )(screened)
    return pl.pallas_call(
        convolve_kernel,
        out_shape=jax.ShapeDtypeStruct((2, energy_count, entries), jnp.float32),
        compiler_params=params,
        in_specs=[whole, whole, whole],
        out_specs=whole,
    )(in_vmem(keep), in_vmem(got), in_vmem(window))


def solution(mesh):
    in_specs = (
        P(None, "space", None, None),
        P(None, "space", None, None),
        P(None, "energy", "space", None, None),
        P(None, None, ("space", "energy")),
    )
    out_specs = P(None, None, ("space", "energy"))
    return jax.shard_map(local, mesh=mesh, in_specs=in_specs, out_specs=out_specs, check_vma=False)
```

```python
import functools

import jax
import jax.numpy as jnp
from jax import lax
from jax.experimental import pallas as pl
from jax.experimental.pallas import tpu as pltpu
from jax.sharding import PartitionSpec as P

broadening = 0.25
energy_low = -3.0
energy_high = 3.0

PANEL = 8
SMALL = 2.0**-48


def iota(shape, dim):
    return lax.broadcasted_iota(jnp.int32, shape, dim)


def swap_halves(x):
    return pltpu.roll(x, x.shape[1] // 2, 1)


def low_half(x):
    return iota(x.shape, 1) < x.shape[1] // 2


def sublane_broadcast(x, row):
    return jnp.broadcast_to(x[row : row + 1, :], x.shape)


def complex_times(a, b):
    return a[0] * b[0] - a[1] * b[1], a[0] * b[1] + a[1] * b[0]


def minus(a, b):
    return a[0] - b[0], a[1] - b[1]


def tree_sum(terms):
    while len(terms) > 1:
        paired = [terms[n] + terms[n + 1] for n in range(0, len(terms) - 1, 2)]
        terms = paired + terms[len(paired) * 2 :]
    return terms[0]


def invert_groups(real, imag, paired):
    real, imag = list(real), list(imag)
    count, shape = len(real), real[0].shape
    half = shape[1] // 2
    lane, sub = iota(shape, 1), iota(shape, 0)
    if paired:
        lane = lane & (half - 1)
    unit = jnp.where((lane & (PANEL - 1)) == sub, 1.0, 0.0)

    def columns(panel, groups):
        found = {group: [] for group in groups}
        for c in range(panel * PANEL, panel * PANEL + PANEL):
            place = (iota(shape, 1) & half) + c
            for group in groups:
                found[group].append(
                    tuple(
                        jnp.take_along_axis(x, place, axis=1, mode="promise_in_bounds")
                        if paired
                        else jnp.broadcast_to(x[:, c : c + 1], shape)
                        for x in (real[group], imag[group])
                    )
                )
        return found

    def spread(pair, row):
        return sublane_broadcast(pair[0], row), sublane_broadcast(pair[1], row)

    block = columns(0, [0])[0]
    for panel in range(count):
        following = (panel + 1) % count
        rest = [group for group in range(count) if group not in (panel, following)]
        inside = (lane // PANEL) == panel
        column = columns(panel, [following])
        column |= columns(panel, rest)
        block = [(a * SMALL, b * SMALL) for a, b in block]
        rows = (jnp.where(inside, unit, real[panel]), jnp.where(inside, 0.0, imag[panel]))
        scale = (jnp.zeros(shape, jnp.float32), jnp.zeros(shape, jnp.float32))
        pivot = spread(block[0], 0)
        for step in range(PANEL):
            here = sub == step
            factor = 1.0 / (pivot[0] * pivot[0] + pivot[1] * pivot[1])
            recip = (pivot[0] * factor, -(pivot[1] * factor))
            if step < PANEL - 1:
                product = complex_times(
                    spread(block[step], step + 1), spread(block[step + 1], step)
                )
                pivot = minus(spread(block[step + 1], step + 1), complex_times(product, recip))
            outer = (jnp.where(here, 0.0, block[step][0]), jnp.where(here, 0.0, block[step][1]))
            multiple = complex_times(outer, recip)
            scale = (jnp.where(here, recip[0], scale[0]), jnp.where(here, recip[1], scale[1]))
            for c in range(step + 1, PANEL):
                block[c] = minus(block[c], complex_times(multiple, spread(block[c], step)))
            rows = minus(rows, complex_times(multiple, spread(rows, step)))
        rows = complex_times(rows, (scale[0] * SMALL, scale[1] * SMALL))
        spreads = [spread(rows, c) for c in range(PANEL)]
        real[panel], imag[panel] = rows
        for group in [following] + rest:
            terms = [complex_times(a, b) for a, b in zip(column[group], spreads)]
            real[group] = jnp.where(inside, 0.0, real[group]) - tree_sum([t[0] for t in terms])
            imag[group] = jnp.where(inside, 0.0, imag[group]) - tree_sum([t[1] for t in terms])
            if group == following and panel < count - 1:
                block = columns(following, [following])[following]
    return real, imag


def invert_pair(first, second, paired=True):
    low = low_half(first)
    real = jnp.where(low, first, swap_halves(second))
    imag = jnp.where(low, swap_halves(first), second)
    groups = first.shape[0] // PANEL
    real = [real[PANEL * g : PANEL * (g + 1)] for g in range(groups)]
    imag = [imag[PANEL * g : PANEL * (g + 1)] for g in range(groups)]
    real, imag = invert_groups(real, imag, paired)
    return jnp.concatenate(real, 0), jnp.concatenate(imag, 0)


def side_of_pair(real, imag):
    low = low_half(real)
    return jnp.where(low, real, swap_halves(imag)), jnp.where(low, swap_halves(real), imag)


def times_i(x):
    turned = swap_halves(x)
    return jnp.where(low_half(x), -turned, turned)


def matmul(a, b):
    a_high, b_high = a.astype(jnp.bfloat16), b.astype(jnp.bfloat16)
    a_low = (a - a_high.astype(jnp.float32)).astype(jnp.bfloat16)
    b_low = (b - b_high.astype(jnp.float32)).astype(jnp.bfloat16)
    return jnp.dot(
        jnp.concatenate([a_high, a_high, a_low], 1),
        jnp.concatenate([b_high, b_low, b_high], 0),
        preferred_element_type=jnp.float32,
    )


def pair_solve(real, imag, right_first, right_second):
    low = low_half(real)
    left = jnp.concatenate(
        [
            jnp.concatenate([jnp.where(low, real, 0.0), jnp.where(low, imag, 0.0)], 1),
            jnp.concatenate([jnp.where(low, 0.0, real), jnp.where(low, 0.0, imag)], 1),
        ],
        0,
    )
    rows = real.shape[0]
    firsts, seconds = [], []
    for a, b in zip(right_first, right_second):
        stacked = jnp.concatenate([a, b], 0)
        turned = times_i(stacked)
        right = jnp.concatenate(
            [
                jnp.concatenate([stacked, turned], 1),
                jnp.concatenate([turned, -stacked], 1),
            ],
            0,
        )
        product = matmul(left, right)
        width = stacked.shape[1]
        firsts.append(jnp.concatenate([product[:rows, :width], product[:rows, width:]], 0))
        seconds.append(jnp.concatenate([product[rows:, :width], product[rows:, width:]], 0))
    return jnp.concatenate(firsts, 1), jnp.concatenate(seconds, 1)


def eliminate(block_first, block_second, sides_first, sides_second):
    real, imag = invert_pair(block_first, block_second)
    right_first, right_second = pair_solve(
        real,
        imag,
        [sides_first[1], sides_first[2]],
        [sides_second[1], sides_second[2]],
    )
    results = []
    for sides, right in ((sides_first, right_first), (sides_second, right_second)):
        rows, width = sides[0].shape
        out = matmul(jnp.concatenate([sides[0], sides[3]], 0), right)
        results.append(
            (out[:rows, :width], out[:rows, width:], out[rows:, :width], out[rows:, width:])
        )
    return results


def eliminate_one(block, sides):
    real, imag = invert_pair(block, sides[1], False)
    inverse, from_left = side_of_pair(real, imag)
    turned = times_i(sides[2])
    rows, width = block.shape
    from_right = matmul(
        inverse,
        jnp.concatenate(
            [jnp.concatenate([sides[2], turned], 1), jnp.concatenate([turned, -sides[2]], 1)], 0
        ),
    )
    right = jnp.concatenate(
        [
            jnp.concatenate([from_left, times_i(from_left)], 0),
            jnp.concatenate([from_right[:, :width], from_right[:, width:]], 0),
        ],
        1,
    )
    out = matmul(jnp.concatenate([sides[0], sides[3]], 0), right)
    return out[:rows, :width], out[:rows, width:], out[rows:, :width], out[rows:, width:]


def adjoint(x):
    half = x.shape[1] // 2
    turned = x.T
    return jnp.concatenate([turned[:half], -turned[half:]], 1)


def reduce_kernel(space_count, energy_count, onsite_ref, hopping_ref, sigma_ref, own_ref, reduced_ref):
    orbitals = onsite_ref.shape[-1]
    level = lax.axis_index("energy").astype(jnp.float32)
    energy = energy_low + (energy_high - energy_low) * (level + 0.5) / energy_count
    active = jnp.where(lax.axis_index("space") < space_count - 1, 1.0, 0.0)
    unit = jnp.where(
        iota((orbitals, orbitals), 0) == iota((orbitals, orbitals), 1), 1.0, 0.0
    )
    system = [
        jnp.concatenate(
            [
                energy * unit - onsite_ref[0, n] - sigma_ref[0, n],
                broadening * unit - onsite_ref[1, n] - sigma_ref[1, n],
            ],
            1,
        )
        for n in range(2)
    ]
    within = jnp.concatenate([hopping_ref[0, 0], hopping_ref[1, 0]], 1)
    beyond = jnp.concatenate([hopping_ref[0, 1], hopping_ref[1, 1]], 1) * active
    within_adjoint, beyond_adjoint = adjoint(within), adjoint(beyond)
    own_ref[0], own_ref[1] = system
    own_ref[2], own_ref[3] = within, within_adjoint
    own_ref[4], own_ref[5] = beyond, beyond_adjoint
    sides = (within, within_adjoint, beyond, beyond_adjoint)
    products = eliminate_one(system[1], sides)
    reduced_ref[0] = system[0] - products[0]
    reduced_ref[1] = products[3]
    reduced_ref[2] = -products[1]
    reduced_ref[3] = -products[2]


def solve_kernel(count, own_ref, *refs):
    flipped, (keep_ref, give_ref, green_ref) = refs[:-3], refs[-3:]
    place = lax.axis_index("space")

    def other(turn, part):
        flips = sorted({r ^ ((r + turn) % count) for r in range(count)})
        wanted = place ^ ((place + turn) & (count - 1))
        value = flipped[flips[0] - 1][part]
        for flip in flips[1:]:
            value = jnp.where(wanted == flip, flipped[flip - 1][part], value)
        return value

    even, odd = own_ref[0], own_ref[1]
    within, within_adjoint = own_ref[2], own_ref[3]
    blocks = {turn: other(turn, 0) for turn in range(1, count)}
    for turn in range(1, count - 1):
        blocks[turn + 1] = blocks[turn + 1] - other(turn, 1)
    blocks[0] = odd
    blocks[count] = even - other(count - 1, 1)
    links = {turn: (other(turn, 2), other(turn, 3)) for turn in range(1, count)}
    links[0] = (-own_ref[4], -own_ref[5])
    stride = 1
    while stride < count:
        turns = list(range(stride, count, 2 * stride))
        last = len(turns) == 1
        for start in range(0, len(turns), 2):
            chosen = turns[start : start + 2]
            sides = [links[t - stride] + links[t] for t in chosen]
            if len(chosen) == 1:
                results = [eliminate_one(blocks[chosen[0]], sides[0])]
            else:
                results = eliminate(blocks[chosen[0]], blocks[chosen[1]], sides[0], sides[1])
            for t, (left_left, left_right, right_left, right_right) in zip(chosen, results):
                blocks[t - stride] = blocks[t - stride] - left_left
                blocks[t + stride] = blocks[t + stride] - right_right
                if not last:
                    links[t - stride] = (-left_right, -right_left)
        stride *= 2
    even, odd = blocks[count], blocks[0]
    inverse, from_odd = side_of_pair(*invert_pair(odd, within_adjoint, False))
    both = matmul(
        within,
        jnp.concatenate(
            [
                jnp.concatenate([from_odd, inverse], 1),
                jnp.concatenate([times_i(from_odd), times_i(inverse)], 1),
            ],
            0,
        ),
    )
    width = even.shape[1]
    first, onward = side_of_pair(*invert_pair(even - both[:, :width], both[:, width:], False))
    second = inverse + matmul(from_odd, jnp.concatenate([onward, times_i(onward)], 0))
    pieces, rows = green_ref.shape[:2]
    for piece in range(pieces // 2):
        green_ref[piece] = first[piece * rows : (piece + 1) * rows]
        green_ref[pieces // 2 + piece] = second[piece * rows : (piece + 1) * rows]
    rank = lax.axis_index("energy")
    for slot in range(pieces // 2):
        keep_ref[slot] = green_ref[rank ^ (2 * slot)]
        give_ref[slot] = green_ref[rank ^ (2 * slot + 1)]


def window_kernel(screened_ref, window_ref, lag_ref):
    sources = window_ref.shape[1]
    lags = screened_ref.shape[1]
    for part in range(2):
        lag_ref[part, : lags - sources] = screened_ref[part, sources:]
        lag_ref[part, lags - sources : lags] = screened_ref[part, :sources]
        for source in range(sources):
            window_ref[part, source] = lag_ref[part, pl.ds(lags - sources - source, sources)]


def exchange_kernel(dests, kept_ref, got_ref, keep_ref, give_ref):
    held = kept_ref.shape[0]
    for source in range(2 * held // dests):
        ref, base = (kept_ref, 0) if source * dests < held else (got_ref, held)
        for dest in range(dests):
            to_ref = give_ref if dest % 2 else keep_ref
            to_ref[(source * dests + dest) // 2] = ref[source * dests + dest - base]


def convolve_kernel(kept_ref, got_ref, window_ref, out_ref):
    half, rows, width = kept_ref.shape
    energies = 2 * half
    low = iota((half, width), 1) < width // 2
    rank = lax.axis_index("energy")
    for tile in range(rows // 2):
        place = pl.ds(tile * width, width)
        terms = []
        for part, ref in enumerate((kept_ref, got_ref)):
            first, second = ref[:, 2 * tile, :], ref[:, 2 * tile + 1, :]
            real = jnp.where(low, first, swap_halves(second))
            imag = jnp.where(low, swap_halves(first), second)
            for n in range(half):
                source = rank ^ (part * half + n)
                green = (
                    jnp.broadcast_to(real[n : n + 1], (energies, width)),
                    jnp.broadcast_to(imag[n : n + 1], (energies, width)),
                )
                screen = (window_ref[0, source, :, place], window_ref[1, source, :, place])
                terms.append(complex_times(green, screen))
        out_ref[0, :, place] = tree_sum([t[0] for t in terms])
        out_ref[1, :, place] = tree_sum([t[1] for t in terms])


def in_vmem(x):
    return pltpu.with_memory_space_constraint(x, pltpu.VMEM)


def local(onsite, hopping, sigma_prior, screened):
    blocks, orbitals = onsite.shape[1], onsite.shape[-1]
    space_count = lax.axis_size("space")
    energy_count = lax.axis_size("energy")
    if blocks != 2 or sigma_prior.shape[1] != 1 or space_count & (space_count - 1):
        raise ValueError("unsupported placement")
    width = 2 * orbitals
    whole = pl.BlockSpec(memory_space=pltpu.VMEM)
    params = pltpu.CompilerParams(vmem_limit_bytes=24 * 2**20)
    own, reduced = pl.pallas_call(
        functools.partial(reduce_kernel, space_count, energy_count),
        out_shape=(
            pltpu.VMEM((6, orbitals, width), jnp.float32),
            pltpu.VMEM((4, orbitals, width), jnp.float32),
        ),
        in_specs=[whole] * 3,
        out_specs=(whole, whole),
    )(onsite, hopping, sigma_prior.reshape(onsite.shape))
    held = {0: reduced}
    bit = space_count // 2
    while bit:
        pairs = [(r, r ^ bit) for r in range(space_count)]
        held |= {flip ^ bit: lax.ppermute(held[flip], "space", pairs) for flip in list(held)}
        bit //= 2
    others = [in_vmem(held[flip]) for flip in range(1, space_count)]
    piece = (blocks * orbitals // energy_count, width)
    halves = (pltpu.VMEM((energy_count // 2,) + piece, jnp.float32),) * 2
    keep, give = pl.pallas_call(
        functools.partial(solve_kernel, space_count),
        out_shape=halves,
        compiler_params=params,
        in_specs=[whole] * space_count,
        out_specs=(whole, whole),
        scratch_shapes=[pltpu.VMEM((energy_count,) + piece, jnp.float32)],
    )(in_vmem(own), *others)
    bit = 1
    while True:
        pairs = [(r, r ^ bit) for r in range(energy_count)]
        got = lax.ppermute(give, "energy", pairs)
        bit *= 2
        if bit == energy_count:
            break
        keep, give = pl.pallas_call(
            functools.partial(exchange_kernel, energy_count // bit),
            out_shape=halves,
            compiler_params=params,
            in_specs=[whole, whole],
            out_specs=(whole, whole),
        )(in_vmem(keep), in_vmem(got))
    lag_count, entries = screened.shape[1:]
    window = pl.pallas_call(
        window_kernel,
        out_shape=pltpu.VMEM((2, energy_count, energy_count, entries), jnp.float32),
        compiler_params=params,
        in_specs=[whole],
        out_specs=whole,
        scratch_shapes=[pltpu.VMEM((2, lag_count + 1, entries), jnp.float32)],
        cost_estimate=pl.CostEstimate(
            flops=0, transcendentals=0, bytes_accessed=16 * energy_count**2 * entries
        ),
    )(screened)
    return pl.pallas_call(
        convolve_kernel,
        out_shape=jax.ShapeDtypeStruct((2, energy_count, entries), jnp.float32),
        compiler_params=params,
        in_specs=[whole, whole, whole],
        out_specs=whole,
    )(in_vmem(keep), in_vmem(got), in_vmem(window))


def solution(mesh):
    in_specs = (
        P(None, "space", None, None),
        P(None, "space", None, None),
        P(None, "energy", "space", None, None),
        P(None, None, ("space", "energy")),
    )
    out_specs = P(None, None, ("space", "energy"))
    return jax.shard_map(local, mesh=mesh, in_specs=in_specs, out_specs=out_specs, check_vma=False)
```

```python
import functools

import jax
import jax.numpy as jnp
from jax import lax
from jax.experimental import pallas as pl
from jax.experimental.pallas import tpu as pltpu
from jax.sharding import PartitionSpec as P

broadening = 0.25
energy_low = -3.0
energy_high = 3.0

PANEL = 8
SMALL = 2.0**-48


def iota(shape, dim):
    return lax.broadcasted_iota(jnp.int32, shape, dim)


def swap_halves(x):
    return pltpu.roll(x, x.shape[1] // 2, 1)


def low_half(x):
    return iota(x.shape, 1) < x.shape[1] // 2


def sublane_broadcast(x, row):
    return jnp.broadcast_to(x[row : row + 1, :], x.shape)


def complex_times(a, b):
    return a[0] * b[0] - a[1] * b[1], a[0] * b[1] + a[1] * b[0]


def minus(a, b):
    return a[0] - b[0], a[1] - b[1]


def tree_sum(terms):
    while len(terms) > 1:
        paired = [terms[n] + terms[n + 1] for n in range(0, len(terms) - 1, 2)]
        terms = paired + terms[len(paired) * 2 :]
    return terms[0]


def invert_groups(real, imag, paired):
    real, imag = list(real), list(imag)
    count, shape = len(real), real[0].shape
    half = shape[1] // 2
    lane, sub = iota(shape, 1), iota(shape, 0)
    if paired:
        lane = lane & (half - 1)
    unit = jnp.where((lane & (PANEL - 1)) == sub, 1.0, 0.0)

    def columns(panel, groups):
        found = {group: [] for group in groups}
        for c in range(panel * PANEL, panel * PANEL + PANEL):
            place = (iota(shape, 1) & half) + c
            for group in groups:
                found[group].append(
                    tuple(
                        jnp.take_along_axis(x, place, axis=1, mode="promise_in_bounds")
                        if paired
                        else jnp.broadcast_to(x[:, c : c + 1], shape)
                        for x in (real[group], imag[group])
                    )
                )
        return found

    def spread(pair, row):
        return sublane_broadcast(pair[0], row), sublane_broadcast(pair[1], row)

    block = columns(0, [0])[0]
    for panel in range(count):
        following = (panel + 1) % count
        rest = [group for group in range(count) if group not in (panel, following)]
        inside = (lane // PANEL) == panel
        column = columns(panel, [following])
        column |= columns(panel, rest)
        block = [(a * SMALL, b * SMALL) for a, b in block]
        rows = (jnp.where(inside, unit, real[panel]), jnp.where(inside, 0.0, imag[panel]))
        scale = (jnp.zeros(shape, jnp.float32), jnp.zeros(shape, jnp.float32))
        pivot = spread(block[0], 0)
        for step in range(PANEL):
            here = sub == step
            factor = 1.0 / (pivot[0] * pivot[0] + pivot[1] * pivot[1])
            recip = (pivot[0] * factor, -(pivot[1] * factor))
            if step < PANEL - 1:
                product = complex_times(
                    spread(block[step], step + 1), spread(block[step + 1], step)
                )
                pivot = minus(spread(block[step + 1], step + 1), complex_times(product, recip))
            outer = (jnp.where(here, 0.0, block[step][0]), jnp.where(here, 0.0, block[step][1]))
            multiple = complex_times(outer, recip)
            scale = (jnp.where(here, recip[0], scale[0]), jnp.where(here, recip[1], scale[1]))
            for c in range(step + 1, PANEL):
                block[c] = minus(block[c], complex_times(multiple, spread(block[c], step)))
            rows = minus(rows, complex_times(multiple, spread(rows, step)))
        rows = complex_times(rows, (scale[0] * SMALL, scale[1] * SMALL))
        spreads = [spread(rows, c) for c in range(PANEL)]
        real[panel], imag[panel] = rows
        for group in [following] + rest:
            terms = [complex_times(a, b) for a, b in zip(column[group], spreads)]
            real[group] = jnp.where(inside, 0.0, real[group]) - tree_sum([t[0] for t in terms])
            imag[group] = jnp.where(inside, 0.0, imag[group]) - tree_sum([t[1] for t in terms])
            if group == following and panel < count - 1:
                block = columns(following, [following])[following]
    return real, imag


def invert_pair(first, second, paired=True):
    low = low_half(first)
    real = jnp.where(low, first, swap_halves(second))
    imag = jnp.where(low, swap_halves(first), second)
    groups = first.shape[0] // PANEL
    real = [real[PANEL * g : PANEL * (g + 1)] for g in range(groups)]
    imag = [imag[PANEL * g : PANEL * (g + 1)] for g in range(groups)]
    real, imag = invert_groups(real, imag, paired)
    return jnp.concatenate(real, 0), jnp.concatenate(imag, 0)


def side_of_pair(real, imag):
    low = low_half(real)
    return jnp.where(low, real, swap_halves(imag)), jnp.where(low, swap_halves(real), imag)


def times_i(x):
    turned = swap_halves(x)
    return jnp.where(low_half(x), -turned, turned)


def matmul(a, b):
    a_high, b_high = a.astype(jnp.bfloat16), b.astype(jnp.bfloat16)
    a_low = (a - a_high.astype(jnp.float32)).astype(jnp.bfloat16)
    b_low = (b - b_high.astype(jnp.float32)).astype(jnp.bfloat16)
    return jnp.dot(
        jnp.concatenate([a_high, a_high, a_low], 1),
        jnp.concatenate([b_high, b_low, b_high], 0),
        preferred_element_type=jnp.float32,
    )


def pair_solve(real, imag, right_first, right_second):
    low = low_half(real)
    left = jnp.concatenate(
        [
            jnp.concatenate([jnp.where(low, real, 0.0), jnp.where(low, imag, 0.0)], 1),
            jnp.concatenate([jnp.where(low, 0.0, real), jnp.where(low, 0.0, imag)], 1),
        ],
        0,
    )
    rows = real.shape[0]
    firsts, seconds = [], []
    for a, b in zip(right_first, right_second):
        stacked = jnp.concatenate([a, b], 0)
        turned = times_i(stacked)
        right = jnp.concatenate(
            [
                jnp.concatenate([stacked, turned], 1),
                jnp.concatenate([turned, -stacked], 1),
            ],
            0,
        )
        product = matmul(left, right)
        width = stacked.shape[1]
        firsts.append(jnp.concatenate([product[:rows, :width], product[:rows, width:]], 0))
        seconds.append(jnp.concatenate([product[rows:, :width], product[rows:, width:]], 0))
    return jnp.concatenate(firsts, 1), jnp.concatenate(seconds, 1)


def eliminate(block_first, block_second, sides_first, sides_second):
    real, imag = invert_pair(block_first, block_second)
    right_first, right_second = pair_solve(
        real,
        imag,
        [sides_first[1], sides_first[2]],
        [sides_second[1], sides_second[2]],
    )
    results = []
    for sides, right in ((sides_first, right_first), (sides_second, right_second)):
        rows, width = sides[0].shape
        out = matmul(jnp.concatenate([sides[0], sides[3]], 0), right)
        results.append(
            (out[:rows, :width], out[:rows, width:], out[rows:, :width], out[rows:, width:])
        )
    return results


def eliminate_one(block, sides):
    real, imag = invert_pair(block, sides[1], False)
    inverse, from_left = side_of_pair(real, imag)
    turned = times_i(sides[2])
    rows, width = block.shape
    from_right = matmul(
        inverse,
        jnp.concatenate(
            [jnp.concatenate([sides[2], turned], 1), jnp.concatenate([turned, -sides[2]], 1)], 0
        ),
    )
    right = jnp.concatenate(
        [
            jnp.concatenate([from_left, times_i(from_left)], 0),
            jnp.concatenate([from_right[:, :width], from_right[:, width:]], 0),
        ],
        1,
    )
    out = matmul(jnp.concatenate([sides[0], sides[3]], 0), right)
    return out[:rows, :width], out[:rows, width:], out[rows:, :width], out[rows:, width:]


def adjoint(x):
    half = x.shape[1] // 2
    turned = x.T
    return jnp.concatenate([turned[:half], -turned[half:]], 1)


def reduce_kernel(space_count, energy_count, onsite_ref, hopping_ref, sigma_ref, own_ref, reduced_ref):
    orbitals = onsite_ref.shape[-1]
    level = lax.axis_index("energy").astype(jnp.float32)
    energy = energy_low + (energy_high - energy_low) * (level + 0.5) / energy_count
    active = jnp.where(lax.axis_index("space") < space_count - 1, 1.0, 0.0)
    unit = jnp.where(
        iota((orbitals, orbitals), 0) == iota((orbitals, orbitals), 1), 1.0, 0.0
    )
    system = [
        jnp.concatenate(
            [
                energy * unit - onsite_ref[0, n] - sigma_ref[0, n],
                broadening * unit - onsite_ref[1, n] - sigma_ref[1, n],
            ],
            1,
        )
        for n in range(2)
    ]
    within = jnp.concatenate([hopping_ref[0, 0], hopping_ref[1, 0]], 1)
    beyond = jnp.concatenate([hopping_ref[0, 1], hopping_ref[1, 1]], 1) * active
    within_adjoint, beyond_adjoint = adjoint(within), adjoint(beyond)
    own_ref[0], own_ref[1] = system
    own_ref[2], own_ref[3] = within, within_adjoint
    own_ref[4], own_ref[5] = beyond, beyond_adjoint
    sides = (within, within_adjoint, beyond, beyond_adjoint)
    products = eliminate_one(system[1], sides)
    reduced_ref[0] = system[0] - products[0]
    reduced_ref[1] = products[3]
    reduced_ref[2] = -products[1]
    reduced_ref[3] = -products[2]


def solve_kernel(count, own_ref, *refs):
    flipped, (keep_ref, give_ref, green_ref) = refs[:-3], refs[-3:]
    place = lax.axis_index("space")

    def other(turn, part):
        flips = sorted({r ^ ((r + turn) % count) for r in range(count)})
        wanted = place ^ ((place + turn) & (count - 1))
        value = flipped[flips[0] - 1][part]
        for flip in flips[1:]:
            value = jnp.where(wanted == flip, flipped[flip - 1][part], value)
        return value

    even, odd = own_ref[0], own_ref[1]
    within, within_adjoint = own_ref[2], own_ref[3]
    blocks = {turn: other(turn, 0) for turn in range(1, count)}
    for turn in range(1, count - 1):
        blocks[turn + 1] = blocks[turn + 1] - other(turn, 1)
    blocks[0] = odd
    blocks[count] = even - other(count - 1, 1)
    links = {turn: (other(turn, 2), other(turn, 3)) for turn in range(1, count)}
    links[0] = (-own_ref[4], -own_ref[5])
    stride = 1
    while stride < count:
        turns = list(range(stride, count, 2 * stride))
        last = len(turns) == 1
        for start in range(0, len(turns), 2):
            chosen = turns[start : start + 2]
            sides = [links[t - stride] + links[t] for t in chosen]
            if len(chosen) == 1:
                results = [eliminate_one(blocks[chosen[0]], sides[0])]
            else:
                results = eliminate(blocks[chosen[0]], blocks[chosen[1]], sides[0], sides[1])
            for t, (left_left, left_right, right_left, right_right) in zip(chosen, results):
                blocks[t - stride] = blocks[t - stride] - left_left
                blocks[t + stride] = blocks[t + stride] - right_right
                if not last:
                    links[t - stride] = (-left_right, -right_left)
        stride *= 2
    even, odd = blocks[count], blocks[0]
    inverse, from_odd = side_of_pair(*invert_pair(odd, within_adjoint, False))
    both = matmul(
        within,
        jnp.concatenate(
            [
                jnp.concatenate([from_odd, inverse], 1),
                jnp.concatenate([times_i(from_odd), times_i(inverse)], 1),
            ],
            0,
        ),
    )
    width = even.shape[1]
    first, onward = side_of_pair(*invert_pair(even - both[:, :width], both[:, width:], False))
    second = inverse + matmul(from_odd, jnp.concatenate([onward, times_i(onward)], 0))
    pieces, rows = green_ref.shape[:2]
    for piece in range(pieces // 2):
        green_ref[piece] = first[piece * rows : (piece + 1) * rows]
        green_ref[pieces // 2 + piece] = second[piece * rows : (piece + 1) * rows]
    rank = lax.axis_index("energy")
    for slot in range(pieces // 2):
        keep_ref[slot] = green_ref[rank ^ (2 * slot)]
        give_ref[slot] = green_ref[rank ^ (2 * slot + 1)]


def window_kernel(screened_ref, window_ref, lag_ref):
    sources = window_ref.shape[1]
    lags = screened_ref.shape[1]
    for part in range(2):
        lag_ref[part, : lags - sources] = screened_ref[part, sources:]
        lag_ref[part, lags - sources : lags] = screened_ref[part, :sources]
        for source in range(sources):
            window_ref[part, source] = lag_ref[part, pl.ds(lags - sources - source, sources)]


def exchange_kernel(dests, kept_ref, got_ref, keep_ref, give_ref):
    held = kept_ref.shape[0]
    for source in range(2 * held // dests):
        ref, base = (kept_ref, 0) if source * dests < held else (got_ref, held)
        for dest in range(dests):
            to_ref = give_ref if dest % 2 else keep_ref
            to_ref[(source * dests + dest) // 2] = ref[source * dests + dest - base]


def convolve_kernel(kept_ref, got_ref, window_ref, out_ref):
    half, rows, width = kept_ref.shape
    energies = 2 * half
    low = iota((half, width), 1) < width // 2
    rank = lax.axis_index("energy")
    for tile in range(rows // 2):
        place = pl.ds(tile * width, width)
        terms = []
        for part, ref in enumerate((kept_ref, got_ref)):
            first, second = ref[:, 2 * tile, :], ref[:, 2 * tile + 1, :]
            real = jnp.where(low, first, swap_halves(second))
            imag = jnp.where(low, swap_halves(first), second)
            for n in range(half):
                source = rank ^ (part * half + n)
                green = (
                    jnp.broadcast_to(real[n : n + 1], (energies, width)),
                    jnp.broadcast_to(imag[n : n + 1], (energies, width)),
                )
                screen = (window_ref[0, source, :, place], window_ref[1, source, :, place])
                terms.append(complex_times(green, screen))
        out_ref[0, :, place] = tree_sum([t[0] for t in terms])
        out_ref[1, :, place] = tree_sum([t[1] for t in terms])


def in_vmem(x):
    return pltpu.with_memory_space_constraint(x, pltpu.VMEM)


def local(onsite, hopping, sigma_prior, screened):
    blocks, orbitals = onsite.shape[1], onsite.shape[-1]
    space_count = lax.axis_size("space")
    energy_count = lax.axis_size("energy")
    if blocks != 2 or sigma_prior.shape[1] != 1 or space_count & (space_count - 1):
        raise ValueError("unsupported placement")
    width = 2 * orbitals
    whole = pl.BlockSpec(memory_space=pltpu.VMEM)
    params = pltpu.CompilerParams(vmem_limit_bytes=24 * 2**20)
    own, reduced = pl.pallas_call(
        functools.partial(reduce_kernel, space_count, energy_count),
        out_shape=(
            pltpu.VMEM((6, orbitals, width), jnp.float32),
            pltpu.VMEM((4, orbitals, width), jnp.float32),
        ),
        in_specs=[whole] * 3,
        out_specs=(whole, whole),
    )(onsite, hopping, sigma_prior.reshape(onsite.shape))
    held = {0: reduced}
    bit = space_count // 2
    while bit:
        pairs = [(r, r ^ bit) for r in range(space_count)]
        held |= {flip ^ bit: lax.ppermute(held[flip], "space", pairs) for flip in list(held)}
        bit //= 2
    others = [in_vmem(held[flip]) for flip in range(1, space_count)]
    piece = (blocks * orbitals // energy_count, width)
    halves = (pltpu.VMEM((energy_count // 2,) + piece, jnp.float32),) * 2
    keep, give = pl.pallas_call(
        functools.partial(solve_kernel, space_count),
        out_shape=halves,
        compiler_params=pltpu.CompilerParams(
            vmem_limit_bytes=24 * 2**20
        ),
        in_specs=[whole] * space_count,
        out_specs=(whole, whole),
        scratch_shapes=[pltpu.VMEM((energy_count,) + piece, jnp.float32)],
    )(in_vmem(own), *others)
    bit = 1
    while True:
        pairs = [(r, r ^ bit) for r in range(energy_count)]
        got = lax.ppermute(give, "energy", pairs)
        bit *= 2
        if bit == energy_count:
            break
        keep, give = pl.pallas_call(
            functools.partial(exchange_kernel, energy_count // bit),
            out_shape=halves,
            compiler_params=params,
            in_specs=[whole, whole],
            out_specs=(whole, whole),
        )(in_vmem(keep), in_vmem(got))
    lag_count, entries = screened.shape[1:]
    window = pl.pallas_call(
        window_kernel,
        out_shape=pltpu.VMEM((2, energy_count, energy_count, entries), jnp.float32),
        compiler_params=params,
        in_specs=[whole],
        out_specs=whole,
        scratch_shapes=[pltpu.VMEM((2, lag_count + 1, entries), jnp.float32)],
        cost_estimate=pl.CostEstimate(
            flops=0, transcendentals=0, bytes_accessed=16 * energy_count**2 * entries
        ),
    )(screened)
    return pl.pallas_call(
        convolve_kernel,
        out_shape=jax.ShapeDtypeStruct((2, energy_count, entries), jnp.float32),
        compiler_params=params,
        in_specs=[whole, whole, whole],
        out_specs=whole,
    )(in_vmem(keep), in_vmem(got), in_vmem(window))


def solution(mesh):
    in_specs = (
        P(None, "space", None, None),
        P(None, "space", None, None),
        P(None, "energy", "space", None, None),
        P(None, None, ("space", "energy")),
    )
    out_specs = P(None, None, ("space", "energy"))
    return jax.shard_map(local, mesh=mesh, in_specs=in_specs, out_specs=out_specs, check_vma=False)
```
